256 devices in a mesh: strip: 8 (over x, core), sub: 32 (over z, y).
Axes of the slice: x: 4, y: 4, z: 8, core: 2. Of those that a mesh axis runs over, the one named last changes fastest.
Arguments:
- node_latents: bfloat16 [65536, 128], P(('strip', 'sub')), may hold values from -6 to 6
- edge_latents: bfloat16 [1048576, 128], P(('strip', 'sub')), may hold values from -6 to 6
- senders: int32 [1048576], P(('strip', 'sub')), may hold values from 0 to 65535, as said below
- receivers: int32 [1048576], P(('strip', 'sub')), may hold values from 0 to 255
- edge_count: int32 [256], P(('strip', 'sub')), may hold values from 1024 to 4096, as said below
- w_edge_in: bfloat16 [384, 128], replicated, may hold values from -0.3125 to 0.3125
- w_edge_out: bfloat16 [128, 128], replicated, may hold values from -0.5 to 0.5
- w_node_in: bfloat16 [256, 128], replicated, may hold values from -0.375 to 0.375
- w_node_out: bfloat16 [128, 128], replicated, may hold values from -0.5 to 0.5
- node_cotangent: bfloat16 [65536, 128], P(('strip', 'sub')), may hold values from -6 to 6
- edge_cotangent: bfloat16 [1048576, 128], P(('strip', 'sub')), may hold values from -6 to 6
Outputs:
- new_nodes: bfloat16 [65536, 128], P(('strip', 'sub'))
- new_edges: bfloat16 [1048576, 128], P(('strip', 'sub'))
- node_grad: float32 [65536, 128], P(('strip', 'sub'))
- grad_edge_in: float32 [384, 128], replicated
- grad_edge_out: float32 [128, 128], replicated
- grad_node_in: float32 [256, 128], replicated
- grad_node_out: float32 [128, 128], replicated
The draws below stay inside these ranges and needn't reach their ends.
Inputs may be any that keep to these rules, and one draw needn't show every extreme that they name: `senders`: devices are numbered strip * 32 + sub-block, each holding 256 consecutive particles and 4096 consecutive edge slots. The sender of an edge held by the device at strip i and sub-block j is a particle of a device at strip i - 1, i or i + 1 and sub-block j - 1, j or j + 1 (no wrap); if that device is not the edge's own, the sender is among its first 32 particles. A device's live edges are its first edge_count slots; some device is full.
All inputs are finite; a program needn't handle non-finite values.
Results may differ from the reference program's by a relative error of at most 0.012.
Values may be sent and summed in bfloat16 or wider, within the bound.
A program may use at most 64 MiB of HBM per device.

```python
import math
import jax
import jax.numpy as jnp
from jax import lax

H = 128
P_DEV = 256
BAND = 32
E_DEV = 4096
STRIPS = 8
SUBS = 32
PARTICLES = 65536
EDGES = 1048576
DEVICES = 256


def draw_senders(key, part):
    key = jax.random.fold_in(key, 11)
    first, second, third, fourth, fifth = jax.random.split(key, 5)
    device = jnp.arange(EDGES, dtype=jnp.int32) // E_DEV
    strip_of = device // SUBS
    sub_of = device % SUBS
    crossing = jax.random.randint(fourth, (EDGES,), 0, 5, dtype=jnp.int32) == 0
    step_strip = jax.random.randint(first, (EDGES,), -1, 2, dtype=jnp.int32)
    step_sub = jax.random.randint(second, (EDGES,), -1, 2, dtype=jnp.int32)
    near_strip = jnp.where(crossing, jnp.clip(strip_of + step_strip, 0, STRIPS - 1), strip_of)
    near_sub = jnp.where(crossing, jnp.clip(sub_of + step_sub, 0, SUBS - 1), sub_of)
    inner = jax.random.randint(third, (EDGES,), 0, P_DEV, dtype=jnp.int32)
    border = jax.random.randint(fifth, (EDGES,), 0, BAND, dtype=jnp.int32)
    local = jnp.where(crossing, border, inner)
    return ((near_strip * SUBS + near_sub) * P_DEV + local).astype(jnp.int32)


def draw_edge_count(key, part):
    key = jax.random.fold_in(key, 23)
    first, second = jax.random.split(key)
    counts = jax.random.randint(first, (DEVICES,), E_DEV // 4, E_DEV + 1, dtype=jnp.int32)
    fullest = jax.random.randint(second, (), 0, DEVICES, dtype=jnp.int32)
    return jnp.where(jnp.arange(DEVICES, dtype=jnp.int32) == fullest, E_DEV, counts).astype(jnp.int32)


def plant(drawn, own_key, least, largest):
    place = [jax.random.randint(jax.random.fold_in(own_key, axis), (), 0, length) for axis, length in enumerate(drawn.shape)]
    main_axis = drawn.shape.index(max(drawn.shape))
    beside = place[:main_axis] + [(place[main_axis] + 1) % drawn.shape[main_axis]] + place[main_axis + 1:]
    return drawn.at[tuple(place)].set(least).at[tuple(beside)].set(largest)


def steps_of(key, dims, cuts, least, top_value):
    loudness = 1.0
    for position, parts in cuts:
        heights = jax.random.uniform(jax.random.fold_in(jax.random.fold_in(key, 6), position), (parts,), jnp.float32, least / len(cuts), top_value / len(cuts))
        loudness = loudness * jnp.repeat(jnp.exp(heights), dims[position] // parts).reshape((-1,) + (1,) * (len(dims) - 1 - position))
    return loudness


def centred(own_key, extent, deviation, reach, shards=(), kind=jnp.bfloat16):
    entries = deviation * jax.random.normal(own_key, extent, jnp.float32)
    if shards:
        entries = entries * steps_of(own_key, extent, shards, -0.22, 0.18)
    return jnp.clip(entries, -reach, reach).astype(kind)


def setup_inputs(seed: int = 0) -> dict:
    key_list = jax.random.split(jax.random.key(seed), 12)
    return {
        "node_latents": centred(key_list[0], (PARTICLES, H), 1.0, 6.0, ((0, 256),)),
        "edge_latents": centred(key_list[1], (EDGES, H), 1.0, 6.0, ((0, 256),)),
        "senders": draw_senders(jax.random.fold_in(key_list[11], 71), 0),
        "receivers": plant(jax.random.randint(key_list[3], (EDGES,), 0, P_DEV), jax.random.fold_in(key_list[3], 1), 0, P_DEV - 1).astype(jnp.int32),
        "edge_count": draw_edge_count(jax.random.fold_in(key_list[11], 71), 0),
        "w_edge_in": centred(key_list[5], (3 * H, H), (3 * H) ** -0.5, 0.3125),
        "w_edge_out": centred(key_list[6], (H, H), H ** -0.5, 0.5),
        "w_node_in": centred(key_list[7], (2 * H, H), (2 * H) ** -0.5, 0.375),
        "w_node_out": centred(key_list[8], (H, H), H ** -0.5, 0.5),
        "node_cotangent": centred(key_list[9], (PARTICLES, H), 1.0, 6.0, ((0, 256),)),
        "edge_cotangent": centred(key_list[10], (EDGES, H), 1.0, 6.0, ((0, 256),)),
    }


EPS = 1e-05

def norm_rows(values):
    centre = values - lax.optimization_barrier(jnp.mean(values, axis=1, keepdims=True))
    scale = lax.rsqrt(lax.optimization_barrier(jnp.mean(centre * centre, axis=1, keepdims=True)) + EPS)
    return (centre * scale, scale)

def norm_back(normed, scale, upstream):
    first = lax.optimization_barrier(jnp.mean(upstream, axis=1, keepdims=True))
    second = lax.optimization_barrier(jnp.mean(upstream * normed, axis=1, keepdims=True))
    return scale * (upstream - first - normed * second)

def silu_grad(values):
    sig = jax.nn.sigmoid(values)
    return sig * (1.0 + values * (1.0 - sig))

def edge_forward(send_rows, recv_rows, edges, valid, w_edge_in, w_edge_out):
    stacked = jnp.concatenate([send_rows, recv_rows, edges], axis=1)
    hidden_pre = jnp.dot(stacked, w_edge_in, preferred_element_type=jnp.float32)
    hidden = jax.nn.silu(hidden_pre).astype(jnp.bfloat16)
    outer = jnp.dot(hidden, w_edge_out, preferred_element_type=jnp.float32)
    normed, scale = norm_rows(outer)
    message = normed * valid[:, None]
    updated = (edges.astype(jnp.float32) + message).astype(jnp.bfloat16)
    return (stacked, hidden_pre, hidden, normed, scale, message, updated)

def edge_back(stacked, hidden_pre, hidden, normed, scale, valid, upstream, w_edge_in, w_edge_out):
    d_outer = norm_back(normed, scale, upstream * valid[:, None]).astype(jnp.bfloat16)
    g_out = jnp.dot(hidden.T, d_outer, preferred_element_type=jnp.float32)
    d_hidden = jnp.dot(d_outer, w_edge_out.T, preferred_element_type=jnp.float32)
    d_pre = (d_hidden * silu_grad(hidden_pre)).astype(jnp.bfloat16)
    g_in = jnp.dot(stacked.T, d_pre, preferred_element_type=jnp.float32)
    d_stacked = jnp.dot(d_pre, w_edge_in.T, preferred_element_type=jnp.float32)
    return (g_in, g_out, d_stacked)

def node_step(nodes, agg_rows, cotangent, w_node_in, w_node_out):
    joined = jnp.concatenate([nodes, agg_rows], axis=1)
    pre = jnp.dot(joined, w_node_in, preferred_element_type=jnp.float32)
    act = jax.nn.silu(pre).astype(jnp.bfloat16)
    outer = jnp.dot(act, w_node_out, preferred_element_type=jnp.float32)
    normed, scale = norm_rows(outer)
    updated = (nodes.astype(jnp.float32) + normed).astype(jnp.bfloat16)
    d_outer = norm_back(normed, scale, cotangent).astype(jnp.bfloat16)
    g_out = jnp.dot(act.T, d_outer, preferred_element_type=jnp.float32)
    d_act = jnp.dot(d_outer, w_node_out.T, preferred_element_type=jnp.float32)
    d_pre = (d_act * silu_grad(pre)).astype(jnp.bfloat16)
    g_in = jnp.dot(joined.T, d_pre, preferred_element_type=jnp.float32)
    d_joined = jnp.dot(d_pre, w_node_in.T, preferred_element_type=jnp.float32)
    return (updated, g_in, g_out, d_joined)

def reference(node_latents, edge_latents, senders, receivers, edge_count, w_edge_in, w_edge_out, w_node_in, w_node_out, node_cotangent, edge_cotangent):
    width = node_latents.shape[1]
    base = jnp.arange(DEVICES, dtype=jnp.int32)[:, None] * P_DEV
    send_blocks = senders.reshape(DEVICES, E_DEV).astype(jnp.int32)
    recv_blocks = (receivers.reshape(DEVICES, E_DEV) + base).astype(jnp.int32)
    edge_blocks = edge_latents.reshape(DEVICES, E_DEV, width)
    cot_blocks = edge_cotangent.reshape(DEVICES, E_DEV, width)
    valid_blocks = (jnp.arange(E_DEV, dtype=jnp.int32)[None, :] < edge_count[:, None]).astype(jnp.float32)

    def forward(agg, item):
        send_idx, recv_idx, edges, valid = item
        out = edge_forward(node_latents[send_idx], node_latents[recv_idx], edges, valid, w_edge_in, w_edge_out)
        return (agg.at[recv_idx].add(out[5]), out[6])
    agg, new_edges = lax.scan(forward, jnp.zeros((PARTICLES, width), jnp.float32), (send_blocks, recv_blocks, edge_blocks, valid_blocks))
    node_cot = node_cotangent.astype(jnp.float32)
    new_nodes, gn_in, gn_out, d_joined = node_step(node_latents, agg.astype(jnp.bfloat16), node_cot, w_node_in, w_node_out)
    d_agg = d_joined[:, width:]

    def backward(carry, item):
        grads, g_in, g_out = carry
        send_idx, recv_idx, edges, valid, cot = item
        out = edge_forward(node_latents[send_idx], node_latents[recv_idx], edges, valid, w_edge_in, w_edge_out)
        upstream = cot.astype(jnp.float32) + d_agg[recv_idx]
        gi, go, d_stacked = edge_back(out[0], out[1], out[2], out[3], out[4], valid, upstream, w_edge_in, w_edge_out)
        grads = grads.at[send_idx].add(d_stacked[:, :width]).at[recv_idx].add(d_stacked[:, width:2 * width])
        return ((grads, g_in + gi, g_out + go), None)
    start = (node_cot + d_joined[:, :width], jnp.zeros(w_edge_in.shape, jnp.float32), jnp.zeros(w_edge_out.shape, jnp.float32))
    (node_grad, ge_in, ge_out), unused = lax.scan(backward, start, (send_blocks, recv_blocks, edge_blocks, valid_blocks, cot_blocks))
    factor = 1.0 / math.sqrt(EDGES)
    return (new_nodes, new_edges.reshape(EDGES, width), node_grad, ge_in * factor, ge_out * factor, gn_in * factor, gn_out * factor)
```

```python
import functools
import math

import jax
import jax.numpy as jnp
from jax import lax
from jax.experimental import pallas as pl
from jax.experimental.pallas import tpu as pltpu
from jax.sharding import PartitionSpec as P

EPS = 1e-05
MESH = pl.DeviceIdType.MESH
F32 = jnp.float32
BF16 = jnp.bfloat16

H = 128
CHUNK = 512
NEAR = [(ds, dj) for ds in (-1, 0, 1) for dj in (-1, 0, 1) if (ds, dj) != (0, 0)]


def dot(a, b):
    return lax.dot_general(a, b, (((1,), (0,)), ((), ())), preferred_element_type=F32)


def dot_nt(a, b):
    return lax.dot_general(a, b, (((1,), (1,)), ((), ())), preferred_element_type=F32)


def dot_tn(a, b):
    return lax.dot_general(a, b, (((0,), (0,)), ((), ())), preferred_element_type=F32)


def split(x):
    high = x.astype(BF16)
    return high, (x - high.astype(F32)).astype(BF16)


def silu_parts(z):
    half = 0.5 * z
    s = 0.5 + 0.5 * jnp.tanh(half)
    a = z * s
    return a, s + a - a * s


def mean_row(x):
    return jnp.mean(x, axis=1, keepdims=True)


def edge_kernel(
    place_ref,
    count_ref,
    nodes_ref,
    halo_ref,
    edges_ref,
    cot_ref,
    send_ref,
    recv_ref,
    w_ei_ref,
    w_eo_ref,
    w_ni_ref,
    w_no_ref,
    ncot_ref,
    new_nodes_ref,
    new_edges_ref,
    local_ref,
    owed_ref,
    grads_ref,
    table_ref,
    sidx_ref,
    weo_ref,
    hotr_ref,
    a1_ref,
    sp_ref,
    n2_ref,
    r2_ref,
    agg_ref,
    dagg_ref,
    gsum_ref,
):
    n_p = nodes_ref.shape[0]
    n_e = edges_ref.shape[0]
    n_h = halo_ref.shape[0]
    border = n_h // 8
    n_s = n_p + n_h
    rows = CHUNK // 128
    steps = n_e // CHUNK
    count = count_ref[0]

    owner = send_ref[...] // n_p
    within = send_ref[...] % n_p
    d_strip = owner // place_ref[2] - place_ref[0]
    d_sub = owner % place_ref[2] - place_ref[1]
    block = (d_strip + 1) * 3 + d_sub + 1
    slot = jnp.where(block > 4, block - 1, block)
    sidx_ref[...] = jnp.where(block == 4, within, n_p + slot * border + (within & (border - 1)))

    table_ref[0:n_p, :] = dot(nodes_ref[...], w_ei_ref[0:H, :]).astype(BF16)
    table_ref[n_p:n_s, :] = dot(halo_ref[...], w_ei_ref[0:H, :]).astype(BF16)
    table_ref[n_s : n_s + n_p, :] = dot(nodes_ref[...], w_ei_ref[H : 2 * H, :]).astype(BF16)
    table_ref[n_s + n_p :, :] = w_ei_ref[2 * H :, :]
    weo = w_eo_ref[...].astype(F32)
    high, low = split(weo - mean_row(weo))
    weo_ref[0:H, :] = high
    weo_ref[H:, :] = low
    agg_ref[...] = jnp.zeros_like(agg_ref)
    gsum_ref[...] = jnp.zeros_like(gsum_ref)

    lane = lax.broadcasted_iota(jnp.int32, (CHUNK, 128), 1)

    def column(ref, c):
        return jnp.concatenate(
            [
                jnp.broadcast_to(ref[pl.ds(c * rows + k, 1), :], (128, 128)).T
                for k in range(rows)
            ],
            axis=0,
        )

    def hot_rows(col, n):
        return jnp.concatenate(
            [(col == lane + k * 128).astype(F32).astype(BF16) for k in range(n // 128)], axis=1
        )

    def hot_cols(ref, c, n):
        sub = lax.broadcasted_iota(jnp.int32, (n, 128), 0)
        return jnp.concatenate(
            [
                (jnp.broadcast_to(ref[pl.ds(c * rows + k, 1), :], (n, 128)) == sub)
                .astype(F32)
                .astype(BF16)
                for k in range(rows)
            ],
            axis=1,
        )

    def forward(c, carry):
        at = pl.ds(pl.multiple_of(c * CHUNK, CHUNK), CHUNK)
        hot_s = hot_rows(column(sidx_ref, c), n_s)
        hot_r = hot_rows(column(recv_ref, c), n_p)
        hotr_ref[at, :] = hot_r
        edges = edges_ref[at, :]
        z1 = dot(jnp.concatenate([hot_s, hot_r, edges], axis=1), table_ref[...])
        a1, sp = silu_parts(z1)
        a1 = a1.astype(BF16)
        a1_ref[at, :] = a1
        sp_ref[at, :] = sp
        centre = dot(jnp.concatenate([a1, a1], axis=1), weo_ref[...])
        r2 = lax.rsqrt(mean_row(centre * centre) + EPS)
        where = c * CHUNK + lax.broadcasted_iota(jnp.int32, (CHUNK, 1), 0)
        r2 = jnp.where(where < count, r2, 0.0)
        n2 = centre * r2
        n2_ref[at, :] = n2
        r2_ref[at, :] = jnp.broadcast_to(r2, (CHUNK, 128))
        new_edges_ref[at, :] = (edges.astype(F32) + n2).astype(BF16)
        agg_ref[...] += dot(hot_cols(recv_ref, c, n_p), n2.astype(BF16))
        return carry

    lax.fori_loop(0, steps, forward, 0)

    nodes = nodes_ref[...]
    joined = jnp.concatenate([nodes, agg_ref[...].astype(BF16)], axis=1)
    a3, sp3 = silu_parts(dot(joined, w_ni_ref[...]))
    a3 = a3.astype(BF16)
    z4 = dot(a3, w_no_ref[...])
    centre = z4 - mean_row(z4)
    r4 = lax.rsqrt(mean_row(centre * centre) + EPS)
    n4 = centre * r4
    new_nodes_ref[...] = (nodes.astype(F32) + n4).astype(BF16)
    ncot = ncot_ref[...].astype(F32)
    dz4 = (r4 * (ncot - mean_row(ncot) - n4 * mean_row(ncot * n4))).astype(BF16)
    dz3 = (dot_nt(dz4, w_no_ref[...]) * sp3).astype(BF16)
    d_joined = dot_nt(dz3, w_ni_ref[...])
    dagg_ref[...] = d_joined[:, H:].astype(BF16)
    local_ref[...] = ncot + d_joined[:, :H]
    grads_ref[4 * H : 6 * H, :] = dot_tn(joined, dz3)
    grads_ref[6 * H : 7 * H, :] = dot_tn(a3, dz4)
    grads_ref[2 * H : 4 * H, :] = jnp.zeros((2 * H, H), F32)

    def backward(c, carry):
        at = pl.ds(pl.multiple_of(c * CHUNK, CHUNK), CHUNK)
        n2 = n2_ref[at, :]
        g = cot_ref[at, :].astype(F32) + dot(hotr_ref[at, :], dagg_ref[...])
        dz2 = (r2_ref[at, :] * (g - mean_row(g) - n2 * mean_row(g * n2))).astype(BF16)
        dz1 = (dot_nt(dz2, w_eo_ref[...]) * sp_ref[at, :]).astype(BF16)
        grads_ref[2 * H : 3 * H, :] += dot_tn(edges_ref[at, :], dz1)
        grads_ref[3 * H : 4 * H, :] += dot_tn(a1_ref[at, :], dz2)
        hot = jnp.concatenate([hot_cols(sidx_ref, c, n_s), hot_cols(recv_ref, c, n_p)], axis=0)
        gsum_ref[...] += dot(hot, dz1)
        return carry

    lax.fori_loop(0, steps, backward, 0)

    g_s = gsum_ref[0:n_s, :].astype(BF16)
    g_r = gsum_ref[n_s:, :].astype(BF16)
    w_s, w_r = w_ei_ref[0:H, :], w_ei_ref[H : 2 * H, :]
    grads_ref[0:H, :] = dot_tn(nodes, g_s[0:n_p, :]) + dot_tn(halo_ref[...], g_s[n_p:, :])
    grads_ref[H : 2 * H, :] = dot_tn(nodes, g_r)
    local_ref[...] += dot_nt(g_s[0:n_p, :], w_s) + dot_nt(g_r, w_r)
    owed_ref[...] = dot_nt(g_s[n_p:, :], w_s).astype(BF16)


def vmem():
    return pl.BlockSpec(memory_space=pltpu.VMEM)


def smem():
    return pl.BlockSpec(memory_space=pltpu.SMEM)


def edge_call(place, count, nodes, halo, edges, cot, send, recv, w_ei, w_eo, w_ni, w_no, ncot):
    n_p, n_h, n_e = nodes.shape[0], halo.shape[0], edges.shape[0]
    n_s = n_p + n_h
    send = send.reshape(n_e // 128, 128)
    recv = recv.reshape(n_e // 128, 128)
    return pl.pallas_call(
        edge_kernel,
        out_shape=(
            jax.ShapeDtypeStruct((n_p, H), BF16),
            jax.ShapeDtypeStruct((n_e, H), BF16),
            jax.ShapeDtypeStruct((n_p, H), F32),
            jax.ShapeDtypeStruct((n_h, H), BF16),
            jax.ShapeDtypeStruct((7 * H, H), F32),
        ),
        in_specs=[smem(), smem()] + [vmem()] * 11,
        out_specs=[vmem()] * 5,
        scratch_shapes=[
            pltpu.VMEM((n_s + n_p + H, H), BF16),
            pltpu.VMEM((n_e // 128, 128), jnp.int32),
            pltpu.VMEM((2 * H, H), BF16),
            pltpu.VMEM((n_e, n_p), BF16),
            pltpu.VMEM((n_e, H), BF16),
            pltpu.VMEM((n_e, H), F32),
            pltpu.VMEM((n_e, H), F32),
            pltpu.VMEM((n_e, H), F32),
            pltpu.VMEM((n_p, H), F32),
            pltpu.VMEM((n_p, H), BF16),
            pltpu.VMEM((n_s + n_p, H), F32),
        ],
        compiler_params=pltpu.CompilerParams(vmem_limit_bytes=48 << 20),
    )(place, count, nodes, halo, edges, cot, send, recv, w_ei, w_eo, w_ni, w_no, ncot)


def around(size_strip, size_sub):
    strip, sub = lax.axis_index("strip"), lax.axis_index("sub")
    return [
        (lax.rem(strip + ds + size_strip, size_strip), lax.rem(sub + dj + size_sub, size_sub))
        for ds, dj in NEAR
    ]


def swap_near(near, pieces, landing, send_sem, recv_sem):
    copies = []
    for k, peer in enumerate(near):
        copies.append(
            pltpu.make_async_remote_copy(
                src_ref=pieces[k],
                dst_ref=landing.at[7 - k],
                send_sem=send_sem.at[k],
                recv_sem=recv_sem.at[7 - k],
                device_id=peer,
                device_id_type=MESH,
            )
        )
    return copies


def greet(peers):
    barrier = pltpu.get_barrier_semaphore()
    for peer in peers:
        pl.semaphore_signal(barrier, inc=1, device_id=peer, device_id_type=MESH)
    pl.semaphore_wait(barrier, len(peers))


def halo_kernel(sizes, rim_ref, out_ref, landing, send_sem, recv_sem):
    near = around(*sizes)
    greet(near)
    copies = swap_near(near, [rim_ref] * 8, landing, send_sem, recv_sem)
    for copy in copies:
        copy.start()
    for copy in copies:
        copy.wait()
    for k in range(8):
        out_ref[k] = landing[k]


def halo_call(sizes, rim):
    border, width = rim.shape
    return pl.pallas_call(
        functools.partial(halo_kernel, sizes),
        out_shape=jax.ShapeDtypeStruct((8, border, width), BF16),
        in_specs=[vmem()],
        out_specs=vmem(),
        scratch_shapes=[
            pltpu.VMEM((8, border, width), BF16),
            pltpu.SemaphoreType.DMA((8,)),
            pltpu.SemaphoreType.DMA((8,)),
        ],
        compiler_params=pltpu.CompilerParams(collective_id=0, has_side_effects=True),
    )(rim)


def total_kernel(
    sizes,
    factor,
    local_ref,
    owed_ref,
    part_ref,
    node_grad_ref,
    total_ref,
    near_land,
    near_send,
    near_recv,
    c_out,
    c_land,
    x_out,
    x_land,
    y_out,
    y_land,
    z_out,
    z_land,
    y_all,
    x_all,
    c_all,
    send_sem,
    recv_sem,
):
    strip, sub = lax.axis_index("strip"), lax.axis_index("sub")
    my_x, my_c = strip // 2, strip % 2
    my_z, my_y = sub // 4, sub % 4
    near = around(*sizes)
    mate = (my_x * 2 + 1 - my_c, sub)
    row_x = [(lax.rem(my_x + d, 4) * 2 + my_c, sub) for d in (1, 2, 3)]
    row_y = [(strip, my_z * 4 + lax.rem(my_y + d, 4)) for d in (1, 2, 3)]
    row_z = [(strip, lax.rem(my_z + d, 8) * 4 + my_y) for d in range(1, 8)]
    greet(near + [mate] + row_x + row_y + row_z)

    def send(src, dst, k, peer):
        copy = pltpu.make_async_remote_copy(
            src_ref=src,
            dst_ref=dst,
            send_sem=send_sem.at[k],
            recv_sem=recv_sem.at[k],
            device_id=peer,
            device_id_type=MESH,
        )
        copy.start()
        return copy

    half = 448
    c_out[...] = part_ref[pl.ds((1 - my_c) * half, half), :].astype(BF16)
    core = send(c_out, c_land, 0, mate)
    returned = swap_near(
        near, [owed_ref.at[k] for k in range(8)], near_land, near_send, near_recv
    )
    for copy in returned:
        copy.start()
    mine = part_ref[pl.ds(my_c * half, half), :]
    core.wait()
    acc = mine + c_land[...].astype(F32)

    x_out[...] = acc.reshape(4, 112, H).astype(BF16)
    copies = [
        send(x_out.at[lax.rem(my_x + d, 4)], x_land.at[d - 1], d, row_x[d - 1]) for d in (1, 2, 3)
    ]
    for copy in copies:
        copy.wait()
    acc = x_out[my_x].astype(F32)
    for d in range(3):
        acc = acc + x_land[d].astype(F32)

    for k in range(4):
        low, high = 32 * k, min(32 * k + 32, 112)
        y_out[k, 0 : high - low, :] = acc[low:high, :].astype(BF16)
    y_out[3, 16:32, :] = jnp.zeros((16, H), BF16)
    copies = [
        send(y_out.at[lax.rem(my_y + d, 4)], y_land.at[d - 1], 3 + d, row_y[d - 1])
        for d in (1, 2, 3)
    ]
    for copy in copies:
        copy.wait()
    acc = y_out[my_y].astype(F32)
    for d in range(3):
        acc = acc + y_land[d].astype(F32)

    z_out[...] = acc.astype(BF16)
    copies = [send(z_out, z_land.at[my_z], 6 + d, row_z[d - 1]) for d in range(1, 8)]
    z_land[my_z] = z_out[...]
    for copy in copies:
        copy.wait()
    acc = z_land[0].astype(F32)
    for k in range(1, 8):
        acc = acc + z_land[k].astype(F32)

    y_all[my_y] = acc.astype(BF16)
    copies = [send(y_all.at[my_y], y_all.at[my_y], 13 + d, row_y[d - 1]) for d in (1, 2, 3)]
    for copy in copies:
        copy.wait()
    x_all[my_x] = y_all[...].reshape(128, H)[0:112, :]
    copies = [send(x_all.at[my_x], x_all.at[my_x], 16 + d, row_x[d - 1]) for d in (1, 2, 3)]
    for copy in copies:
        copy.wait()
    c_all[my_c] = x_all[...].reshape(half, H)
    core = send(c_all.at[my_c], c_all.at[my_c], 20, mate)
    core.wait()
    total_ref[...] = c_all[...].reshape(2 * half, H).astype(F32) * factor

    for copy in returned:
        copy.wait()
    back = near_land[0].astype(F32)
    for k in range(1, 8):
        back = back + near_land[k].astype(F32)
    border = back.shape[0]
    node_grad_ref[...] = local_ref[...]
    node_grad_ref[0:border, :] += back


def total_call(sizes, factor, local, owed, part):
    border = owed.shape[1]
    return pl.pallas_call(
        functools.partial(total_kernel, sizes, factor),
        out_shape=(
            jax.ShapeDtypeStruct(local.shape, F32),
            jax.ShapeDtypeStruct(part.shape, F32),
        ),
        in_specs=[vmem()] * 3,
        out_specs=[vmem()] * 2,
        scratch_shapes=[
            pltpu.VMEM((8, border, H), BF16),
            pltpu.SemaphoreType.DMA((8,)),
            pltpu.SemaphoreType.DMA((8,)),
            pltpu.VMEM((448, H), BF16),
            pltpu.VMEM((448, H), BF16),
            pltpu.VMEM((4, 112, H), BF16),
            pltpu.VMEM((3, 112, H), BF16),
            pltpu.VMEM((4, 32, H), BF16),
            pltpu.VMEM((3, 32, H), BF16),
            pltpu.VMEM((32, H), BF16),
            pltpu.VMEM((8, 32, H), BF16),
            pltpu.VMEM((4, 32, H), BF16),
            pltpu.VMEM((4, 112, H), BF16),
            pltpu.VMEM((2, 448, H), BF16),
            pltpu.SemaphoreType.DMA((21,)),
            pltpu.SemaphoreType.DMA((21,)),
        ],
        compiler_params=pltpu.CompilerParams(collective_id=1, has_side_effects=True),
    )(local, owed, part)


def shards(
    node_latents,
    edge_latents,
    senders,
    receivers,
    edge_count,
    w_edge_in,
    w_edge_out,
    w_node_in,
    w_node_out,
    node_cotangent,
    edge_cotangent,
):
    count_p = node_latents.shape[0]
    count_e = edge_latents.shape[0]
    border = count_p // 8
    sizes = (lax.axis_size("strip"), lax.axis_size("sub"))
    factor = 1.0 / math.sqrt(count_e * sizes[0] * sizes[1])
    place = jnp.stack(
        [lax.axis_index("strip"), lax.axis_index("sub"), jnp.int32(sizes[1])]
    ).astype(jnp.int32)
    halo = halo_call(sizes, node_latents[:border])
    new_nodes, new_edges, local, owed, part = edge_call(
        place,
        edge_count,
        node_latents,
        halo.reshape(8 * border, H),
        edge_latents,
        edge_cotangent,
        senders,
        receivers,
        w_edge_in,
        w_edge_out,
        w_node_in,
        w_node_out,
        node_cotangent,
    )
    node_grad, total = total_call(sizes, factor, local, owed.reshape(8, border, H), part)
    return (
        new_nodes,
        new_edges,
        node_grad,
        total[: 3 * H],
        total[3 * H : 4 * H],
        total[4 * H : 6 * H],
        total[6 * H :],
    )


def solution(mesh):
    placed = (
        P(("strip", "sub"), None),
        P(("strip", "sub"), None),
        P(("strip", "sub")),
        P(("strip", "sub")),
        P(("strip", "sub")),
        P(),
        P(),
        P(),
        P(),
        P(("strip", "sub"), None),
        P(("strip", "sub"), None),
    )
    return jax.shard_map(
        shards,
        mesh=mesh,
        in_specs=placed,
        out_specs=(
            P(("strip", "sub"), None),
            P(("strip", "sub"), None),
            P(("strip", "sub"), None),
            P(),
            P(),
            P(),
            P(),
        ),
        check_vma=False,
    )
```

```python
import functools
import math

import jax
import jax.numpy as jnp
from jax import lax
from jax.experimental import pallas as pl
from jax.experimental.pallas import tpu as pltpu
from jax.sharding import PartitionSpec as P

EPS = 1e-05
MESH = pl.DeviceIdType.MESH
F32 = jnp.float32
BF16 = jnp.bfloat16

H = 128
CHUNK = 2048
WIDE = 2048
NEAR = [(ds, dj) for ds in (-1, 0, 1) for dj in (-1, 0, 1) if (ds, dj) != (0, 0)]


def dot(a, b):
    return lax.dot_general(a, b, (((1,), (0,)), ((), ())), preferred_element_type=F32)


def dot_nt(a, b):
    return lax.dot_general(a, b, (((1,), (1,)), ((), ())), preferred_element_type=F32)


def dot_tn(a, b):
    return lax.dot_general(a, b, (((0,), (0,)), ((), ())), preferred_element_type=F32)


def split(x):
    high = x.astype(BF16)
    return high, (x - high.astype(F32)).astype(BF16)


def silu_parts(z):
    half = 0.5 * z
    s = 0.5 + 0.5 * jnp.tanh(half)
    a = z * s
    return a, s + a - a * s


def mean_row(x):
    return jnp.mean(x, axis=1, keepdims=True)


def around(sizes):
    strip, sub = lax.axis_index("strip"), lax.axis_index("sub")
    return [
        (lax.rem(strip + ds + sizes[0], sizes[0]), lax.rem(sub + dj + sizes[1], sizes[1]))
        for ds, dj in NEAR
    ]


def remote(src, dst, send_sem, recv_sem, peer):
    return pltpu.make_async_remote_copy(
        src_ref=src,
        dst_ref=dst,
        send_sem=send_sem,
        recv_sem=recv_sem,
        device_id=peer,
        device_id_type=MESH,
    )


def step_kernel(
    sizes,
    nodes_hbm,
    edges_hbm,
    send_hbm,
    recv_hbm,
    count_hbm,
    w_ei_hbm,
    w_eo_hbm,
    w_ni_hbm,
    w_no_hbm,
    ncot_hbm,
    cot_hbm,
    new_nodes_hbm,
    new_edges_hbm,
    node_grad_hbm,
    total_hbm,
    nodes_ref,
    edges_ref,
    send_ref,
    recv_ref,
    count_ref,
    w_ei_ref,
    w_eo_ref,
    w_ni_ref,
    w_no_ref,
    ncot_ref,
    cot_ref,
    load_sem,
    new_nodes_ref,
    new_edges_ref,
    node_grad_ref,
    store_sem,
    halo_ref,
    owed_ref,
    back_ref,
    near_sem,
    table_ref,
    sidx_ref,
    weo_ref,
    hot_ref,
    z1_ref,
    a1_ref,
    sp_ref,
    n2_ref,
    r2_ref,
    agg_ref,
    dagg_ref,
    gsum_ref,
    part_ref,
    c_out,
    c_land,
    x_out,
    x_land,
    y_out,
    y_land,
    z_out,
    z_land,
    y_all,
    x_all,
    c_all,
    send_sem,
    recv_sem,
):
    n_p = nodes_ref.shape[0]
    n_e = edges_ref.shape[0]
    border = halo_ref.shape[1]
    n_h = 8 * border
    n_l = 2 * n_p + H
    strip, sub = lax.axis_index("strip"), lax.axis_index("sub")
    my_x, my_c = strip // 2, strip % 2
    my_z, my_y = sub // 4, sub % 4
    near = around(sizes)
    mate = (my_x * 2 + 1 - my_c, sub)
    row_x = [(lax.rem(my_x + d, 4) * 2 + my_c, sub) for d in (1, 2, 3)]
    row_y = [(strip, my_z * 4 + lax.rem(my_y + d, 4)) for d in (1, 2, 3)]
    row_z = [(strip, lax.rem(my_z + d, 8) * 4 + my_y) for d in range(1, 8)]
    peers = near + [mate] + row_x + row_y + row_z

    pairs = [
        (nodes_hbm, nodes_ref),
        (w_ei_hbm, w_ei_ref),
        (send_hbm, send_ref),
        (recv_hbm, recv_ref),
        (w_eo_hbm, w_eo_ref),
        (edges_hbm, edges_ref),
        (count_hbm, count_ref),
        (w_ni_hbm, w_ni_ref),
        (w_no_hbm, w_no_ref),
        (ncot_hbm, ncot_ref),
        (cot_hbm, cot_ref),
    ]
    loads = [pltpu.make_async_copy(a, b, load_sem.at[k]) for k, (a, b) in enumerate(pairs)]
    for load in loads:
        load.start()
    barrier = pltpu.get_barrier_semaphore()
    for peer in peers:
        pl.semaphore_signal(barrier, inc=1, device_id=peer, device_id_type=MESH)

    loads[0].wait()
    loads[1].wait()
    nodes = nodes_ref[...]
    table_ref[0:n_p, :] = dot(nodes, w_ei_ref[0:H, :]).astype(BF16)
    table_ref[n_p : 2 * n_p, :] = dot(nodes, w_ei_ref[H : 2 * H, :]).astype(BF16)
    table_ref[2 * n_p : n_l, :] = w_ei_ref[2 * H :, :]

    loads[2].wait()
    owner = send_ref[...] // n_p
    within = send_ref[...] % n_p
    d_strip = owner // sizes[1] - strip
    d_sub = owner % sizes[1] - sub
    block = (d_strip + 1) * 3 + d_sub + 1
    slot = jnp.where(block > 4, block - 1, block)
    sidx_ref[...] = jnp.where(block == 4, within, n_p + slot * border + (within & (border - 1)))
    loads[4].wait()
    weo = w_eo_ref[...].astype(F32)
    high, low = split(weo - mean_row(weo))
    weo_ref[0:H, :] = high
    weo_ref[H:, :] = low
    agg_ref[...] = jnp.zeros_like(agg_ref)
    gsum_ref[...] = jnp.zeros_like(gsum_ref)
    part_ref[2 * H : 4 * H, :] = jnp.zeros((2 * H, H), F32)

    pl.semaphore_wait(barrier, len(peers))
    halo_copies = [
        remote(
            nodes_ref.at[pl.ds(0, border), :],
            halo_ref.at[7 - k],
            near_sem.at[0, k],
            near_sem.at[1, 7 - k],
            peer,
        )
        for k, peer in enumerate(near)
    ]
    for copy in halo_copies:
        copy.start()

    def column(ref, c, size):
        rows = size // 128
        return jnp.concatenate(
            [
                jnp.broadcast_to(ref[pl.ds(c * rows + k, 1), :], (128, 128)).T.astype(jnp.int16)
                for k in range(rows)
            ],
            axis=0,
        )

    def hot_rows(col, first, n):
        size = col.shape[0]
        lane = lax.broadcasted_iota(jnp.int32, (size, 128), 1).astype(jnp.int16)
        one, zero = jnp.ones((size, 128), BF16), jnp.zeros((size, 128), BF16)
        return [
            jnp.where(col == lane + jnp.int16(first + k * 128), one, zero)
            for k in range(n // 128)
        ]

    def hot_cols(ref, c, size, n):
        rows = size // 128
        down = lax.broadcasted_iota(jnp.int32, (n, 128), 0).astype(jnp.int16)
        one, zero = jnp.ones((n, 128), BF16), jnp.zeros((n, 128), BF16)
        return jnp.concatenate(
            [
                jnp.where(
                    jnp.broadcast_to(ref[pl.ds(c * rows + k, 1), :], (n, 128)).astype(jnp.int16)
                    == down,
                    one,
                    zero,
                )
                for k in range(rows)
            ],
            axis=1,
        )

    loads[3].wait()
    loads[5].wait()

    def local_part(c, carry):
        at = pl.ds(pl.multiple_of(c * WIDE, WIDE), WIDE)
        col = column(sidx_ref, c, WIDE)
        hot_s = hot_rows(col, 0, n_p)
        hot_h = hot_rows(col, n_p, n_h)
        hot_r = hot_rows(column(recv_ref, c, WIDE), 0, n_p)
        hot_ref[at, :] = jnp.concatenate(hot_h + hot_r, axis=1)
        z1_ref[at, :] = dot(
            jnp.concatenate(hot_s + hot_r + [edges_ref[at, :]], axis=1), table_ref[0:n_l, :]
        )
        return carry

    lax.fori_loop(0, n_e // WIDE, local_part, 0)

    for copy in halo_copies:
        copy.wait()
    halo = halo_ref[...].reshape(n_h, H)
    table_ref[n_l:, :] = dot(halo, w_ei_ref[0:H, :]).astype(BF16)
    loads[6].wait()
    count = count_ref[0]

    def forward(c, carry):
        at = pl.ds(pl.multiple_of(c * CHUNK, CHUNK), CHUNK)
        z1 = z1_ref[at, :] + dot(hot_ref[at, 0:n_h], table_ref[n_l:, :])
        a1, sp = silu_parts(z1)
        a1 = a1.astype(BF16)
        a1_ref[at, :] = a1
        sp_ref[at, :] = sp
        centre = dot(jnp.concatenate([a1, a1], axis=1), weo_ref[...])
        r2 = lax.rsqrt(mean_row(centre * centre) + EPS)
        where = c * CHUNK + lax.broadcasted_iota(jnp.int32, (CHUNK, 1), 0)
        r2 = jnp.where(where < count, r2, 0.0)
        n2 = centre * r2
        n2_ref[at, :] = n2
        r2_ref[at, :] = jnp.broadcast_to(r2, (CHUNK, 128))
        new_edges_ref[at, :] = (edges_ref[at, :].astype(F32) + n2).astype(BF16)
        agg_ref[...] += dot(hot_cols(recv_ref, c, CHUNK, n_p), n2.astype(BF16))
        return carry

    lax.fori_loop(0, n_e // CHUNK, forward, 0)

    stores = [pltpu.make_async_copy(new_edges_ref, new_edges_hbm, store_sem.at[0])]
    stores[0].start()
    for k in (7, 8, 9):
        loads[k].wait()
    joined = jnp.concatenate([nodes, agg_ref[...].astype(BF16)], axis=1)
    a3, sp3 = silu_parts(dot(joined, w_ni_ref[...]))
    a3 = a3.astype(BF16)
    z4 = dot(a3, w_no_ref[...])
    centre = z4 - mean_row(z4)
    r4 = lax.rsqrt(mean_row(centre * centre) + EPS)
    n4 = centre * r4
    new_nodes_ref[...] = (nodes.astype(F32) + n4).astype(BF16)
    ncot = ncot_ref[...].astype(F32)
    dz4 = (r4 * (ncot - mean_row(ncot) - n4 * mean_row(ncot * n4))).astype(BF16)
    dz3 = (dot_nt(dz4, w_no_ref[...]) * sp3).astype(BF16)
    d_joined = dot_nt(dz3, w_ni_ref[...])
    dagg_ref[...] = d_joined[:, H:].astype(BF16)
    node_grad_ref[...] = ncot + d_joined[:, :H]
    part_ref[4 * H : 6 * H, :] = dot_tn(joined, dz3)
    part_ref[6 * H : 7 * H, :] = dot_tn(a3, dz4)
    stores.append(pltpu.make_async_copy(new_nodes_ref, new_nodes_hbm, store_sem.at[1]))
    stores[1].start()
    loads[10].wait()

    def backward(c, carry):
        at = pl.ds(pl.multiple_of(c * CHUNK, CHUNK), CHUNK)
        n2 = n2_ref[at, :]
        g = cot_ref[at, :].astype(F32) + dot(hot_ref[at, n_h:], dagg_ref[...])
        dz2 = (r2_ref[at, :] * (g - mean_row(g) - n2 * mean_row(g * n2))).astype(BF16)
        dz1 = (dot_nt(dz2, w_eo_ref[...]) * sp_ref[at, :]).astype(BF16)
        part_ref[2 * H : 3 * H, :] += dot_tn(edges_ref[at, :], dz1)
        part_ref[3 * H : 4 * H, :] += dot_tn(a1_ref[at, :], dz2)
        hot = jnp.concatenate(
            [hot_cols(sidx_ref, c, CHUNK, n_p + n_h), hot_cols(recv_ref, c, CHUNK, n_p)], axis=0
        )
        gsum_ref[...] += dot(hot, dz1)
        return carry

    lax.fori_loop(0, n_e // CHUNK, backward, 0)

    g_s = gsum_ref[0:n_p, :].astype(BF16)
    g_h = gsum_ref[n_p : n_p + n_h, :].astype(BF16)
    g_r = gsum_ref[n_p + n_h :, :].astype(BF16)
    w_s, w_r = w_ei_ref[0:H, :], w_ei_ref[H : 2 * H, :]
    part_ref[0:H, :] = dot_tn(nodes, g_s) + dot_tn(halo, g_h)
    part_ref[H : 2 * H, :] = dot_tn(nodes, g_r)

    half = c_out.shape[0]
    c_out[...] = part_ref[pl.ds((1 - my_c) * half, half), :].astype(BF16)
    core = remote(c_out, c_land, send_sem.at[0], recv_sem.at[0], mate)
    core.start()
    owed_ref[...] = dot_nt(g_h, w_s).astype(BF16).reshape(8, border, H)
    returned = [
        remote(owed_ref.at[k], back_ref.at[7 - k], near_sem.at[2, k], near_sem.at[3, 7 - k], peer)
        for k, peer in enumerate(near)
    ]
    for copy in returned:
        copy.start()
    node_grad_ref[...] += dot_nt(g_s, w_s) + dot_nt(g_r, w_r)
    mine = part_ref[pl.ds(my_c * half, half), :]
    core.wait()
    acc = mine + c_land[...].astype(F32)

    def share(src, dst, base, row):
        copies = [
            remote(src(d), dst(d), send_sem.at[base + d], recv_sem.at[base + d], peer)
            for d, peer in enumerate(row, 1)
        ]
        for copy in copies:
            copy.start()
        return copies

    piece = half // 4
    x_out[...] = acc.reshape(4, piece, H).astype(BF16)
    copies = share(lambda d: x_out.at[lax.rem(my_x + d, 4)], lambda d: x_land.at[d - 1], 0, row_x)
    for copy in copies:
        copy.wait()
    acc = x_out[my_x].astype(F32)
    for d in range(3):
        acc = acc + x_land[d].astype(F32)

    for k in range(4):
        low, high = 32 * k, min(32 * k + 32, piece)
        y_out[k, 0 : high - low, :] = acc[low:high, :].astype(BF16)
    y_out[3, 16:32, :] = jnp.zeros((16, H), BF16)
    copies = share(lambda d: y_out.at[lax.rem(my_y + d, 4)], lambda d: y_land.at[d - 1], 3, row_y)
    for copy in copies:
        copy.wait()
    acc = y_out[my_y].astype(F32)
    for d in range(3):
        acc = acc + y_land[d].astype(F32)

    z_out[...] = acc.astype(BF16)
    copies = share(lambda d: z_out, lambda d: z_land.at[my_z], 6, row_z)
    z_land[my_z] = z_out[...]

    for copy in returned:
        copy.wait()
    back = back_ref[0].astype(F32)
    for k in range(1, 8):
        back = back + back_ref[k].astype(F32)
    node_grad_ref[0:border, :] += back
    stores.append(pltpu.make_async_copy(node_grad_ref, node_grad_hbm, store_sem.at[2]))
    stores[2].start()

    for copy in copies:
        copy.wait()
    acc = z_land[0].astype(F32)
    for k in range(1, 8):
        acc = acc + z_land[k].astype(F32)

    y_all[my_y] = acc.astype(BF16)
    copies = share(lambda d: y_all.at[my_y], lambda d: y_all.at[my_y], 13, row_y)
    for copy in copies:
        copy.wait()
    x_all[my_x] = y_all[...].reshape(128, H)[0:piece, :]
    copies = share(lambda d: x_all.at[my_x], lambda d: x_all.at[my_x], 16, row_x)
    for copy in copies:
        copy.wait()
    c_all[my_c] = x_all[...].reshape(half, H)
    core = remote(c_all.at[my_c], c_all.at[my_c], send_sem.at[20], recv_sem.at[20], mate)
    core.start()
    core.wait()
    stores.append(pltpu.make_async_copy(c_all, total_hbm, store_sem.at[3]))
    stores[3].start()
    for store in stores:
        store.wait()


def vmem():
    return pl.BlockSpec(memory_space=pltpu.VMEM)


def hbm():
    return pl.BlockSpec(memory_space=pltpu.HBM)


def anywhere():
    return pl.BlockSpec(memory_space=pl.ANY)


def step_call(sizes, args):
    n_p, n_e = args[0].shape[0], args[1].shape[0]
    border = n_p // 8
    n_h = 8 * border
    half = 7 * H // 2
    dma = pltpu.SemaphoreType.DMA
    return pl.pallas_call(
        functools.partial(step_kernel, sizes),
        out_shape=(
            jax.ShapeDtypeStruct((n_p, H), BF16),
            jax.ShapeDtypeStruct((n_e, H), BF16),
            jax.ShapeDtypeStruct((n_p, H), F32),
            jax.ShapeDtypeStruct((2, half, H), BF16),
        ),
        in_specs=[hbm()] * 11,
        out_specs=[hbm()] * 4,
        scratch_shapes=[
            pltpu.SMEM(a.shape, a.dtype) if a.shape == (1,) else pltpu.VMEM(a.shape, a.dtype)
            for a in args
        ]
        + [
            dma((11,)),
            pltpu.VMEM((n_p, H), BF16),
            pltpu.VMEM((n_e, H), BF16),
            pltpu.VMEM((n_p, H), F32),
            dma((4,)),
            pltpu.VMEM((8, border, H), BF16),
            pltpu.VMEM((8, border, H), BF16),
            pltpu.VMEM((8, border, H), BF16),
            dma((4, 8)),
            pltpu.VMEM((2 * n_p + H + n_h, H), BF16),
            pltpu.VMEM((n_e // 128, 128), jnp.int32),
            pltpu.VMEM((2 * H, H), BF16),
            pltpu.VMEM((n_e, n_h + n_p), BF16),
            pltpu.VMEM((n_e, H), F32),
            pltpu.VMEM((n_e, H), BF16),
            pltpu.VMEM((n_e, H), F32),
            pltpu.VMEM((n_e, H), F32),
            pltpu.VMEM((n_e, H), F32),
            pltpu.VMEM((n_p, H), F32),
            pltpu.VMEM((n_p, H), BF16),
            pltpu.VMEM((2 * n_p + n_h, H), F32),
            pltpu.VMEM((7 * H, H), F32),
            pltpu.VMEM((half, H), BF16),
            pltpu.VMEM((half, H), BF16),
            pltpu.VMEM((4, half // 4, H), BF16),
            pltpu.VMEM((3, half // 4, H), BF16),
            pltpu.VMEM((4, 32, H), BF16),
            pltpu.VMEM((3, 32, H), BF16),
            pltpu.VMEM((32, H), BF16),
            pltpu.VMEM((8, 32, H), BF16),
            pltpu.VMEM((4, 32, H), BF16),
            pltpu.VMEM((4, half // 4, H), BF16),
            pltpu.VMEM((2, half, H), BF16),
            dma((21,)),
            dma((21,)),
        ],
        compiler_params=pltpu.CompilerParams(
            collective_id=0, has_side_effects=True, vmem_limit_bytes=62_000_000
        ),
    )(*args)


def finish_kernel(
    factor,
    nn_ref,
    ne_ref,
    ng_ref,
    total_ref,
    nn_out,
    ne_out,
    ng_out,
    ei_out,
    eo_out,
    ni_out,
    no_out,
    nn_buf,
    ne_buf,
    ng_buf,
    total_buf,
    grad_buf,
    in_sem,
    out_sem,
):
    quarter = ne_buf.shape[0] // 4
    parts = [pl.ds(k * quarter, quarter) for k in range(4)]
    brought = [pltpu.make_async_copy(total_ref, total_buf, in_sem.at[0])]
    for k, part in enumerate(parts):
        brought.append(
            pltpu.make_async_copy(ne_ref.at[part, :], ne_buf.at[part, :], in_sem.at[1 + k])
        )
    brought.append(pltpu.make_async_copy(ng_ref, ng_buf, in_sem.at[5]))
    brought.append(pltpu.make_async_copy(nn_ref, nn_buf, in_sem.at[6]))
    for copy in brought:
        copy.start()
    taken = []

    def take(src, dst):
        taken.append(pltpu.make_async_copy(src, dst, out_sem.at[len(taken)]))
        taken[-1].start()

    brought[0].wait()
    half = total_buf.shape[1]
    grad_buf[0:half, :] = total_buf[0].astype(F32) * factor
    grad_buf[half:, :] = total_buf[1].astype(F32) * factor
    first = 0
    for out in (ei_out, eo_out, ni_out, no_out):
        take(grad_buf.at[pl.ds(first, out.shape[0]), :], out)
        first += out.shape[0]
    for k, part in enumerate(parts):
        brought[1 + k].wait()
        take(ne_buf.at[part, :], ne_out.at[part, :])
    brought[5].wait()
    take(ng_buf, ng_out)
    brought[6].wait()
    take(nn_buf, nn_out)
    for copy in taken:
        copy.wait()


def finish_call(factor, new_nodes, new_edges, node_grad, total):
    shapes = [
        (new_nodes.shape, BF16),
        (new_edges.shape, BF16),
        (node_grad.shape, F32),
        ((3 * H, H), F32),
        ((H, H), F32),
        ((2 * H, H), F32),
        ((H, H), F32),
    ]
    return pl.pallas_call(
        functools.partial(finish_kernel, factor),
        out_shape=tuple(jax.ShapeDtypeStruct(s, t) for s, t in shapes),
        in_specs=[hbm()] * 4,
        out_specs=[hbm()] * 7,
        scratch_shapes=[
            pltpu.VMEM(new_nodes.shape, BF16),
            pltpu.VMEM(new_edges.shape, BF16),
            pltpu.VMEM(node_grad.shape, F32),
            pltpu.VMEM(total.shape, BF16),
            pltpu.VMEM((7 * H, H), F32),
            pltpu.SemaphoreType.DMA((7,)),
            pltpu.SemaphoreType.DMA((10,)),
        ],
        compiler_params=pltpu.CompilerParams(vmem_limit_bytes=62_000_000),
    )(new_nodes, new_edges, node_grad, total)


def shards(
    node_latents,
    edge_latents,
    senders,
    receivers,
    edge_count,
    w_edge_in,
    w_edge_out,
    w_node_in,
    w_node_out,
    node_cotangent,
    edge_cotangent,
):
    count_e = edge_latents.shape[0]
    sizes = (lax.axis_size("strip"), lax.axis_size("sub"))
    factor = 1.0 / math.sqrt(count_e * sizes[0] * sizes[1])
    return finish_call(
        factor,
        *step_call(
            sizes,
            (
                node_latents,
                edge_latents,
                senders.reshape(count_e // 128, 128),
                receivers.reshape(count_e // 128, 128),
                edge_count,
                w_edge_in,
                w_edge_out,
                w_node_in,
                w_node_out,
                node_cotangent,
                edge_cotangent,
            ),
        )
    )


def solution(mesh):
    placed = (
        P(("strip", "sub"), None),
        P(("strip", "sub"), None),
        P(("strip", "sub")),
        P(("strip", "sub")),
        P(("strip", "sub")),
        P(),
        P(),
        P(),
        P(),
        P(("strip", "sub"), None),
        P(("strip", "sub"), None),
    )
    return jax.shard_map(
        shards,
        mesh=mesh,
        in_specs=placed,
        out_specs=(
            P(("strip", "sub"), None),
            P(("strip", "sub"), None),
            P(("strip", "sub"), None),
            P(),
            P(),
            P(),
            P(),
        ),
        check_vma=False,
    )
```

```python
import functools
import math

import jax
import jax.numpy as jnp
from jax import lax
from jax.experimental import pallas as pl
from jax.experimental.pallas import tpu as pltpu
from jax.sharding import PartitionSpec as P

EPS = 1e-05
MESH = pl.DeviceIdType.MESH
F32 = jnp.float32
BF16 = jnp.bfloat16

H = 128
CHUNK = 2048
WIDE = 2048
PIECES = [(112 * (k // 4) + 32 * (k % 4), 16 if k % 4 == 3 else 32) for k in range(16)]
HOPS = [min(d // 4, 4 - d // 4) + min(d % 4, 4 - d % 4) for d in range(16)]
FROM_NEAR = sorted(range(1, 16), key=lambda d: HOPS[d])
NEAR = [(ds, dj) for ds in (-1, 0, 1) for dj in (-1, 0, 1) if (ds, dj) != (0, 0)]


def dot(a, b):
    return lax.dot_general(a, b, (((1,), (0,)), ((), ())), preferred_element_type=F32)


def dot_nt(a, b):
    return lax.dot_general(a, b, (((1,), (1,)), ((), ())), preferred_element_type=F32)


def dot_tn(a, b):
    return lax.dot_general(a, b, (((0,), (0,)), ((), ())), preferred_element_type=F32)


def split(x):
    high = x.astype(BF16)
    return high, (x - high.astype(F32)).astype(BF16)


def silu_parts(z):
    half = 0.5 * z
    s = 0.5 + 0.5 * jnp.tanh(half)
    a = z * s
    return a, s + a - a * s


def mean_row(x):
    return jnp.mean(x, axis=1, keepdims=True)


def around(sizes):
    strip, sub = lax.axis_index("strip"), lax.axis_index("sub")
    return [
        (lax.rem(strip + ds + sizes[0], sizes[0]), lax.rem(sub + dj + sizes[1], sizes[1]))
        for ds, dj in NEAR
    ]


def remote(src, dst, send_sem, recv_sem, peer):
    return pltpu.make_async_remote_copy(
        src_ref=src,
        dst_ref=dst,
        send_sem=send_sem,
        recv_sem=recv_sem,
        device_id=peer,
        device_id_type=MESH,
    )


def step_kernel(
    sizes,
    nodes_hbm,
    edges_hbm,
    send_hbm,
    recv_hbm,
    count_hbm,
    w_ei_hbm,
    w_eo_hbm,
    w_ni_hbm,
    w_no_hbm,
    ncot_hbm,
    cot_hbm,
    new_nodes_hbm,
    new_edges_hbm,
    node_grad_hbm,
    total_hbm,
    nodes_ref,
    edges_ref,
    send_ref,
    recv_ref,
    count_ref,
    w_ei_ref,
    w_eo_ref,
    w_ni_ref,
    w_no_ref,
    ncot_ref,
    cot_ref,
    load_sem,
    new_nodes_ref,
    new_edges_ref,
    node_grad_ref,
    store_sem,
    halo_ref,
    owed_ref,
    back_ref,
    near_sem,
    table_ref,
    sidx_ref,
    weo_ref,
    hot_ref,
    z1_ref,
    a1_ref,
    sp_ref,
    n2_ref,
    r2_ref,
    agg_ref,
    dagg_ref,
    gsum_ref,
    part_ref,
    c_out,
    c_land,
    p_out,
    p_land,
    z_out,
    z_land,
    all_ref,
    send_sem,
    recv_sem,
):
    n_p = nodes_ref.shape[0]
    n_e = edges_ref.shape[0]
    border = halo_ref.shape[1]
    n_h = 8 * border
    n_l = 2 * n_p + H
    strip, sub = lax.axis_index("strip"), lax.axis_index("sub")
    my_x, my_c = strip // 2, strip % 2
    my_z, my_y = sub // 4, sub % 4
    near = around(sizes)
    mate = (my_x * 2 + 1 - my_c, sub)

    def shifted(dx, dy):
        return lax.rem(my_x + dx, 4), lax.rem(my_y + dy, 4)

    plane = [shifted(d // 4, d % 4) for d in range(1, 16)]
    origin = [shifted(4 - d // 4, 4 - d % 4) for d in range(1, 16)]
    plane_row = [(x * 2 + my_c, my_z * 4 + y) for x, y in plane]
    row_z = [(strip, lax.rem(my_z + d, 8) * 4 + my_y) for d in range(1, 8)]
    peers = near + [mate] + plane_row + row_z

    pairs = [
        (nodes_hbm, nodes_ref),
        (w_ei_hbm, w_ei_ref),
        (send_hbm, send_ref),
        (recv_hbm, recv_ref),
        (w_eo_hbm, w_eo_ref),
        (edges_hbm, edges_ref),
        (count_hbm, count_ref),
        (w_ni_hbm, w_ni_ref),
        (w_no_hbm, w_no_ref),
        (ncot_hbm, ncot_ref),
        (cot_hbm, cot_ref),
    ]
    loads = [pltpu.make_async_copy(a, b, load_sem.at[k]) for k, (a, b) in enumerate(pairs)]
    for load in loads:
        load.start()
    barrier = pltpu.get_barrier_semaphore()
    for peer in peers:
        pl.semaphore_signal(barrier, inc=1, device_id=peer, device_id_type=MESH)

    loads[0].wait()
    loads[1].wait()
    nodes = nodes_ref[...]
    table_ref[0:n_p, :] = dot(nodes, w_ei_ref[0:H, :]).astype(BF16)
    table_ref[n_p : 2 * n_p, :] = dot(nodes, w_ei_ref[H : 2 * H, :]).astype(BF16)
    table_ref[2 * n_p : n_l, :] = w_ei_ref[2 * H :, :]

    loads[2].wait()
    owner = send_ref[...] // n_p
    within = send_ref[...] % n_p
    d_strip = owner // sizes[1] - strip
    d_sub = owner % sizes[1] - sub
    block = (d_strip + 1) * 3 + d_sub + 1
    slot = jnp.where(block > 4, block - 1, block)
    sidx_ref[...] = jnp.where(block == 4, within, n_p + slot * border + (within & (border - 1)))
    loads[4].wait()
    weo = w_eo_ref[...].astype(F32)
    high, low = split(weo - mean_row(weo))
    weo_ref[0:H, :] = high
    weo_ref[H:, :] = low
    agg_ref[...] = jnp.zeros_like(agg_ref)
    gsum_ref[...] = jnp.zeros_like(gsum_ref)
    part_ref[2 * H : 4 * H, :] = jnp.zeros((2 * H, H), F32)
    for k in (3, 7, 11, 15):
        p_out[k, 16:32, :] = jnp.zeros((16, H), BF16)

    pl.semaphore_wait(barrier, len(peers))
    halo_copies = [
        remote(
            nodes_ref.at[pl.ds(0, border), :],
            halo_ref.at[7 - k],
            near_sem.at[0, k],
            near_sem.at[1, 7 - k],
            peer,
        )
        for k, peer in enumerate(near)
    ]
    for copy in halo_copies:
        copy.start()

    def column(ref, c, size):
        rows = size // 128
        return jnp.concatenate(
            [
                jnp.broadcast_to(ref[pl.ds(c * rows + k, 1), :], (128, 128)).T.astype(jnp.int16)
                for k in range(rows)
            ],
            axis=0,
        )

    def hot_rows(col, first, n):
        size = col.shape[0]
        lane = lax.broadcasted_iota(jnp.int32, (size, 128), 1).astype(jnp.int16)
        one, zero = jnp.ones((size, 128), BF16), jnp.zeros((size, 128), BF16)
        return [
            jnp.where(col == lane + jnp.int16(first + k * 128), one, zero)
            for k in range(n // 128)
        ]

    def hot_cols(ref, c, size, n):
        rows = size // 128
        down = lax.broadcasted_iota(jnp.int32, (n, 128), 0).astype(jnp.int16)
        one, zero = jnp.ones((n, 128), BF16), jnp.zeros((n, 128), BF16)
        return jnp.concatenate(
            [
                jnp.where(
                    jnp.broadcast_to(ref[pl.ds(c * rows + k, 1), :], (n, 128)).astype(jnp.int16)
                    == down,
                    one,
                    zero,
                )
                for k in range(rows)
            ],
            axis=1,
        )

    loads[3].wait()
    loads[5].wait()

    def local_part(c, carry):
        at = pl.ds(pl.multiple_of(c * WIDE, WIDE), WIDE)
        col = column(sidx_ref, c, WIDE)
        hot_s = hot_rows(col, 0, n_p)
        hot_h = hot_rows(col, n_p, n_h)
        hot_r = hot_rows(column(recv_ref, c, WIDE), 0, n_p)
        hot_ref[at, :] = jnp.concatenate(hot_h + hot_r, axis=1)
        z1_ref[at, :] = dot(
            jnp.concatenate(hot_s + hot_r + [edges_ref[at, :]], axis=1), table_ref[0:n_l, :]
        )
        return carry

    lax.fori_loop(0, n_e // WIDE, local_part, 0)

    for copy in halo_copies:
        copy.wait()
    halo = halo_ref[...].reshape(n_h, H)
    table_ref[n_l:, :] = dot(halo, w_ei_ref[0:H, :]).astype(BF16)
    loads[6].wait()
    count = count_ref[0]

    def forward(c, carry):
        at = pl.ds(pl.multiple_of(c * CHUNK, CHUNK), CHUNK)
        z1 = z1_ref[at, :] + dot(hot_ref[at, 0:n_h], table_ref[n_l:, :])
        a1, sp = silu_parts(z1)
        a1 = a1.astype(BF16)
        a1_ref[at, :] = a1
        sp_ref[at, :] = sp
        centre = dot(jnp.concatenate([a1, a1], axis=1), weo_ref[...])
        r2 = lax.rsqrt(mean_row(centre * centre) + EPS)
        where = c * CHUNK + lax.broadcasted_iota(jnp.int32, (CHUNK, 1), 0)
        r2 = jnp.where(where < count, r2, 0.0)
        n2 = centre * r2
        n2_ref[at, :] = n2
        r2_ref[at, :] = jnp.broadcast_to(r2, (CHUNK, 128))
        new_edges_ref[at, :] = (edges_ref[at, :].astype(F32) + n2).astype(BF16)
        agg_ref[...] += dot(hot_cols(recv_ref, c, CHUNK, n_p), n2.astype(BF16))
        return carry

    lax.fori_loop(0, n_e // CHUNK, forward, 0)

    stores = [pltpu.make_async_copy(new_edges_ref, new_edges_hbm, store_sem.at[0])]
    stores[0].start()
    for k in (7, 8, 9):
        loads[k].wait()
    joined = jnp.concatenate([nodes, agg_ref[...].astype(BF16)], axis=1)
    a3, sp3 = silu_parts(dot(joined, w_ni_ref[...]))
    a3 = a3.astype(BF16)
    z4 = dot(a3, w_no_ref[...])
    centre = z4 - mean_row(z4)
    r4 = lax.rsqrt(mean_row(centre * centre) + EPS)
    n4 = centre * r4
    new_nodes_ref[...] = (nodes.astype(F32) + n4).astype(BF16)
    ncot = ncot_ref[...].astype(F32)
    dz4 = (r4 * (ncot - mean_row(ncot) - n4 * mean_row(ncot * n4))).astype(BF16)
    dz3 = (dot_nt(dz4, w_no_ref[...]) * sp3).astype(BF16)
    d_joined = dot_nt(dz3, w_ni_ref[...])
    dagg_ref[...] = d_joined[:, H:].astype(BF16)
    node_grad_ref[...] = ncot + d_joined[:, :H]
    part_ref[4 * H : 6 * H, :] = dot_tn(joined, dz3)
    part_ref[6 * H : 7 * H, :] = dot_tn(a3, dz4)
    stores.append(pltpu.make_async_copy(new_nodes_ref, new_nodes_hbm, store_sem.at[1]))
    stores[1].start()
    loads[10].wait()

    def backward(c, carry):
        at = pl.ds(pl.multiple_of(c * CHUNK, CHUNK), CHUNK)
        n2 = n2_ref[at, :]
        g = cot_ref[at, :].astype(F32) + dot(hot_ref[at, n_h:], dagg_ref[...])
        dz2 = (r2_ref[at, :] * (g - mean_row(g) - n2 * mean_row(g * n2))).astype(BF16)
        dz1 = (dot_nt(dz2, w_eo_ref[...]) * sp_ref[at, :]).astype(BF16)
        part_ref[2 * H : 3 * H, :] += dot_tn(edges_ref[at, :], dz1)
        part_ref[3 * H : 4 * H, :] += dot_tn(a1_ref[at, :], dz2)
        hot = jnp.concatenate(
            [hot_cols(sidx_ref, c, CHUNK, n_p + n_h), hot_cols(recv_ref, c, CHUNK, n_p)], axis=0
        )
        gsum_ref[...] += dot(hot, dz1)
        return carry

    lax.fori_loop(0, n_e // CHUNK, backward, 0)

    g_s = gsum_ref[0:n_p, :].astype(BF16)
    g_h = gsum_ref[n_p : n_p + n_h, :].astype(BF16)
    g_r = gsum_ref[n_p + n_h :, :].astype(BF16)
    w_s, w_r = w_ei_ref[0:H, :], w_ei_ref[H : 2 * H, :]
    part_ref[0:H, :] = dot_tn(nodes, g_s) + dot_tn(halo, g_h)
    part_ref[H : 2 * H, :] = dot_tn(nodes, g_r)

    half = c_out.shape[0]
    c_out[...] = part_ref[pl.ds((1 - my_c) * half, half), :].astype(BF16)
    core = remote(c_out, c_land, send_sem.at[0], recv_sem.at[0], mate)
    core.start()
    owed_ref[...] = dot_nt(g_h, w_s).astype(BF16).reshape(8, border, H)
    returned = [
        remote(owed_ref.at[k], back_ref.at[7 - k], near_sem.at[2, k], near_sem.at[3, 7 - k], peer)
        for k, peer in enumerate(near)
    ]
    for copy in returned:
        copy.start()
    node_grad_ref[...] += dot_nt(g_s, w_s) + dot_nt(g_r, w_r)
    core.wait()

    def share(src, dst, base, row):
        copies = [
            remote(src(d), dst(d), send_sem.at[base + d], recv_sem.at[base + d], peer)
            for d, peer in enumerate(row, 1)
        ]
        for copy in copies:
            copy.start()
        return copies

    for k, (low, size) in enumerate(PIECES):
        mine = part_ref[pl.ds(my_c * half + low, size), :]
        p_out[k, 0:size, :] = (mine + c_land[low : low + size, :].astype(F32)).astype(BF16)
    my_p = my_x * 4 + my_y
    copies = share(
        lambda d: p_out.at[plane[d - 1][0] * 4 + plane[d - 1][1]],
        lambda d: p_land.at[d - 1],
        0,
        plane_row,
    )
    acc = p_out[my_p].astype(F32)
    for d in FROM_NEAR:
        copies[d - 1].wait()
        acc = acc + p_land[d - 1].astype(F32)

    z_out[...] = acc.astype(BF16)
    copies = share(lambda d: z_out, lambda d: z_land.at[my_z], 15, row_z)
    z_land[my_z] = z_out[...]

    for copy in returned:
        copy.wait()
    back = back_ref[0].astype(F32)
    for k in range(1, 8):
        back = back + back_ref[k].astype(F32)
    node_grad_ref[0:border, :] += back
    stores.append(pltpu.make_async_copy(node_grad_ref, node_grad_hbm, store_sem.at[2]))
    stores[2].start()

    for copy in copies:
        copy.wait()
    acc = z_land[0].astype(F32)
    for k in range(1, 8):
        acc = acc + z_land[k].astype(F32)

    def pass_on(k, p):
        piece = all_ref.at[my_c, p]
        copy = remote(piece, piece, send_sem.at[38 + k], recv_sem.at[38 + k], mate)
        copy.start()
        return copy

    all_ref[my_c, my_p] = acc.astype(BF16)
    copies = share(
        lambda d: all_ref.at[my_c, my_p], lambda d: all_ref.at[my_c, my_p], 22, plane_row
    )
    passed = [pass_on(0, my_p)]
    for d in FROM_NEAR:
        copies[d - 1].wait()
        passed.append(pass_on(d, origin[d - 1][0] * 4 + origin[d - 1][1]))
    for copy in passed:
        copy.wait()
    stores.append(pltpu.make_async_copy(all_ref, total_hbm, store_sem.at[3]))
    stores[3].start()
    for store in stores:
        store.wait()


def vmem():
    return pl.BlockSpec(memory_space=pltpu.VMEM)


def hbm():
    return pl.BlockSpec(memory_space=pltpu.HBM)


def anywhere():
    return pl.BlockSpec(memory_space=pl.ANY)


def step_call(sizes, args):
    n_p, n_e = args[0].shape[0], args[1].shape[0]
    border = n_p // 8
    n_h = 8 * border
    half = 7 * H // 2
    dma = pltpu.SemaphoreType.DMA
    return pl.pallas_call(
        functools.partial(step_kernel, sizes),
        out_shape=(
            jax.ShapeDtypeStruct((n_p, H), BF16),
            jax.ShapeDtypeStruct((n_e, H), BF16),
            jax.ShapeDtypeStruct((n_p, H), F32),
            jax.ShapeDtypeStruct((2, 16, 32, H), BF16),
        ),
        in_specs=[hbm()] * 11,
        out_specs=[hbm()] * 4,
        scratch_shapes=[
            pltpu.SMEM(a.shape, a.dtype) if a.shape == (1,) else pltpu.VMEM(a.shape, a.dtype)
            for a in args
        ]
        + [
            dma((11,)),
            pltpu.VMEM((n_p, H), BF16),
            pltpu.VMEM((n_e, H), BF16),
            pltpu.VMEM((n_p, H), F32),
            dma((4,)),
            pltpu.VMEM((8, border, H), BF16),
            pltpu.VMEM((8, border, H), BF16),
            pltpu.VMEM((8, border, H), BF16),
            dma((4, 8)),
            pltpu.VMEM((2 * n_p + H + n_h, H), BF16),
            pltpu.VMEM((n_e // 128, 128), jnp.int32),
            pltpu.VMEM((2 * H, H), BF16),
            pltpu.VMEM((n_e, n_h + n_p), BF16),
            pltpu.VMEM((n_e, H), F32),
            pltpu.VMEM((n_e, H), BF16),
            pltpu.VMEM((n_e, H), F32),
            pltpu.VMEM((n_e, H), F32),
            pltpu.VMEM((n_e, H), F32),
            pltpu.VMEM((n_p, H), F32),
            pltpu.VMEM((n_p, H), BF16),
            pltpu.VMEM((2 * n_p + n_h, H), F32),
            pltpu.VMEM((7 * H, H), F32),
            pltpu.VMEM((half, H), BF16),
            pltpu.VMEM((half, H), BF16),
            pltpu.VMEM((16, 32, H), BF16),
            pltpu.VMEM((15, 32, H), BF16),
            pltpu.VMEM((32, H), BF16),
            pltpu.VMEM((8, 32, H), BF16),
            pltpu.VMEM((2, 16, 32, H), BF16),
            dma((54,)),
            dma((54,)),
        ],
        compiler_params=pltpu.CompilerParams(
            collective_id=0, has_side_effects=True, vmem_limit_bytes=62_000_000
        ),
    )(*args)


def finish_kernel(
    factor,
    nn_ref,
    ne_ref,
    ng_ref,
    total_ref,
    nn_out,
    ne_out,
    ng_out,
    ei_out,
    eo_out,
    ni_out,
    no_out,
    nn_buf,
    ne_buf,
    ng_buf,
    total_buf,
    grad_buf,
    in_sem,
    out_sem,
):
    quarter = ne_buf.shape[0] // 4
    parts = [pl.ds(k * quarter, quarter) for k in range(4)]
    brought = [pltpu.make_async_copy(total_ref, total_buf, in_sem.at[0])]
    for k, part in enumerate(parts):
        brought.append(
            pltpu.make_async_copy(ne_ref.at[part, :], ne_buf.at[part, :], in_sem.at[1 + k])
        )
    brought.append(pltpu.make_async_copy(ng_ref, ng_buf, in_sem.at[5]))
    brought.append(pltpu.make_async_copy(nn_ref, nn_buf, in_sem.at[6]))
    for copy in brought:
        copy.start()
    taken = []

    def take(src, dst):
        taken.append(pltpu.make_async_copy(src, dst, out_sem.at[len(taken)]))
        taken[-1].start()

    brought[0].wait()
    half = grad_buf.shape[0] // 2
    for c in range(2):
        for k, (low, size) in enumerate(PIECES):
            rows = pl.ds(c * half + low, size)
            grad_buf[rows, :] = total_buf[c, k, 0:size, :].astype(F32) * factor
    first = 0
    for out in (ei_out, eo_out, ni_out, no_out):
        take(grad_buf.at[pl.ds(first, out.shape[0]), :], out)
        first += out.shape[0]
    for k, part in enumerate(parts):
        brought[1 + k].wait()
        take(ne_buf.at[part, :], ne_out.at[part, :])
    brought[5].wait()
    take(ng_buf, ng_out)
    brought[6].wait()
    take(nn_buf, nn_out)
    for copy in taken:
        copy.wait()


def finish_call(factor, new_nodes, new_edges, node_grad, total):
    shapes = [
        (new_nodes.shape, BF16),
        (new_edges.shape, BF16),
        (node_grad.shape, F32),
        ((3 * H, H), F32),
        ((H, H), F32),
        ((2 * H, H), F32),
        ((H, H), F32),
    ]
    return pl.pallas_call(
        functools.partial(finish_kernel, factor),
        out_shape=tuple(jax.ShapeDtypeStruct(s, t) for s, t in shapes),
        in_specs=[hbm()] * 4,
        out_specs=[hbm()] * 7,
        scratch_shapes=[
            pltpu.VMEM(new_nodes.shape, BF16),
            pltpu.VMEM(new_edges.shape, BF16),
            pltpu.VMEM(node_grad.shape, F32),
            pltpu.VMEM(total.shape, BF16),
            pltpu.VMEM((7 * H, H), F32),
            pltpu.SemaphoreType.DMA((7,)),
            pltpu.SemaphoreType.DMA((10,)),
        ],
        compiler_params=pltpu.CompilerParams(vmem_limit_bytes=62_000_000),
    )(new_nodes, new_edges, node_grad, total)


def shards(
    node_latents,
    edge_latents,
    senders,
    receivers,
    edge_count,
    w_edge_in,
    w_edge_out,
    w_node_in,
    w_node_out,
    node_cotangent,
    edge_cotangent,
):
    count_e = edge_latents.shape[0]
    sizes = (lax.axis_size("strip"), lax.axis_size("sub"))
    factor = 1.0 / math.sqrt(count_e * sizes[0] * sizes[1])
    return finish_call(
        factor,
        *step_call(
            sizes,
            (
                node_latents,
                edge_latents,
                senders.reshape(count_e // 128, 128),
                receivers.reshape(count_e // 128, 128),
                edge_count,
                w_edge_in,
                w_edge_out,
                w_node_in,
                w_node_out,
                node_cotangent,
                edge_cotangent,
            ),
        )
    )


def solution(mesh):
    placed = (
        P(("strip", "sub"), None),
        P(("strip", "sub"), None),
        P(("strip", "sub")),
        P(("strip", "sub")),
        P(("strip", "sub")),
        P(),
        P(),
        P(),
        P(),
        P(("strip", "sub"), None),
        P(("strip", "sub"), None),
    )
    return jax.shard_map(
        shards,
        mesh=mesh,
        in_specs=placed,
        out_specs=(
            P(("strip", "sub"), None),
            P(("strip", "sub"), None),
            P(("strip", "sub"), None),
            P(),
            P(),
            P(),
            P(),
        ),
        check_vma=False,
    )
```

```python
import functools
import math

import jax
import jax.numpy as jnp
from jax import lax
from jax.experimental import pallas as pl
from jax.experimental.pallas import tpu as pltpu
from jax.sharding import PartitionSpec as P

EPS = 1e-05
MESH = pl.DeviceIdType.MESH
F32 = jnp.float32
BF16 = jnp.bfloat16

H = 128
CHUNK = 2048
WIDE = 2048
PIECES = [(112 * (k // 4) + 32 * (k % 4), 16 if k % 4 == 3 else 32) for k in range(16)]
HOPS = [min(d // 4, 4 - d // 4) + min(d % 4, 4 - d % 4) for d in range(16)]
FROM_NEAR = sorted(range(1, 16), key=lambda d: HOPS[d])
SHIFTS = (2, 1, 3, 0)
NEAR = [(ds, dj) for ds in (-1, 0, 1) for dj in (-1, 0, 1) if (ds, dj) != (0, 0)]


def dot(a, b):
    return lax.dot_general(a, b, (((1,), (0,)), ((), ())), preferred_element_type=F32)


def dot_nt(a, b):
    return lax.dot_general(a, b, (((1,), (1,)), ((), ())), preferred_element_type=F32)


def dot_tn(a, b):
    return lax.dot_general(a, b, (((0,), (0,)), ((), ())), preferred_element_type=F32)


def split(x):
    high = x.astype(BF16)
    return high, (x - high.astype(F32)).astype(BF16)


def silu_parts(z):
    half = 0.5 * z
    s = 0.5 + 0.5 * jnp.tanh(half)
    a = z * s
    return a, s + a - a * s


def mean_row(x):
    return jnp.mean(x, axis=1, keepdims=True)


def around(sizes):
    strip, sub = lax.axis_index("strip"), lax.axis_index("sub")
    return [
        (lax.rem(strip + ds + sizes[0], sizes[0]), lax.rem(sub + dj + sizes[1], sizes[1]))
        for ds, dj in NEAR
    ]


def remote(src, dst, send_sem, recv_sem, peer):
    return pltpu.make_async_remote_copy(
        src_ref=src,
        dst_ref=dst,
        send_sem=send_sem,
        recv_sem=recv_sem,
        device_id=peer,
        device_id_type=MESH,
    )


def step_kernel(
    sizes,
    nodes_hbm,
    edges_hbm,
    send_hbm,
    recv_hbm,
    count_hbm,
    w_ei_hbm,
    w_eo_hbm,
    w_ni_hbm,
    w_no_hbm,
    ncot_hbm,
    cot_hbm,
    new_nodes_hbm,
    new_edges_hbm,
    node_grad_hbm,
    total_hbm,
    nodes_ref,
    edges_ref,
    send_ref,
    recv_ref,
    count_ref,
    w_ei_ref,
    w_eo_ref,
    w_ni_ref,
    w_no_ref,
    ncot_ref,
    cot_ref,
    load_sem,
    new_nodes_ref,
    new_edges_ref,
    node_grad_ref,
    store_sem,
    halo_ref,
    owed_ref,
    back_ref,
    near_sem,
    table_ref,
    sidx_ref,
    weo_ref,
    hot_ref,
    z1_ref,
    a1_ref,
    sp_ref,
    n2_ref,
    r2_ref,
    agg_ref,
    dagg_ref,
    gsum_ref,
    part_ref,
    c_out,
    c_land,
    p_out,
    p_land,
    z_out,
    z_land,
    all_ref,
    send_sem,
    recv_sem,
):
    n_p = nodes_ref.shape[0]
    n_e = edges_ref.shape[0]
    border = halo_ref.shape[1]
    n_h = 8 * border
    n_l = 2 * n_p + H
    strip, sub = lax.axis_index("strip"), lax.axis_index("sub")
    my_x, my_c = strip // 2, strip % 2
    my_z, my_y = sub // 4, sub % 4
    near = around(sizes)
    mate = (my_x * 2 + 1 - my_c, sub)

    def shifted(dx, dy):
        return lax.rem(my_x + dx, 4), lax.rem(my_y + dy, 4)

    plane = [shifted(d // 4, d % 4) for d in range(1, 16)]
    origin = [shifted(4 - d // 4, 4 - d % 4) for d in range(1, 16)]
    plane_row = [(x * 2 + my_c, my_z * 4 + y) for x, y in plane]
    row_z = [(strip, lax.rem(my_z + d, 8) * 4 + my_y) for d in range(1, 8)]
    peers = near + [mate] + plane_row + row_z

    pairs = [
        (nodes_hbm, nodes_ref),
        (w_ei_hbm, w_ei_ref),
        (send_hbm, send_ref),
        (recv_hbm, recv_ref),
        (w_eo_hbm, w_eo_ref),
        (edges_hbm, edges_ref),
        (count_hbm, count_ref),
        (w_ni_hbm, w_ni_ref),
        (w_no_hbm, w_no_ref),
        (ncot_hbm, ncot_ref),
        (cot_hbm, cot_ref),
    ]
    loads = [pltpu.make_async_copy(a, b, load_sem.at[k]) for k, (a, b) in enumerate(pairs)]
    for load in loads:
        load.start()
    barrier = pltpu.get_barrier_semaphore()
    for peer in peers:
        pl.semaphore_signal(barrier, inc=1, device_id=peer, device_id_type=MESH)

    loads[0].wait()
    loads[1].wait()
    nodes = nodes_ref[...]
    table_ref[0:n_p, :] = dot(nodes, w_ei_ref[0:H, :]).astype(BF16)
    table_ref[n_p : 2 * n_p, :] = dot(nodes, w_ei_ref[H : 2 * H, :]).astype(BF16)
    table_ref[2 * n_p : n_l, :] = w_ei_ref[2 * H :, :]

    loads[2].wait()
    owner = send_ref[...] // n_p
    within = send_ref[...] % n_p
    d_strip = owner // sizes[1] - strip
    d_sub = owner % sizes[1] - sub
    block = (d_strip + 1) * 3 + d_sub + 1
    slot = jnp.where(block > 4, block - 1, block)
    sidx_ref[...] = jnp.where(block == 4, within, n_p + slot * border + (within & (border - 1)))
    loads[4].wait()
    weo = w_eo_ref[...].astype(F32)
    high, low = split(weo - mean_row(weo))
    weo_ref[0:H, :] = high
    weo_ref[H:, :] = low
    agg_ref[...] = jnp.zeros_like(agg_ref)
    gsum_ref[...] = jnp.zeros_like(gsum_ref)
    part_ref[2 * H : 4 * H, :] = jnp.zeros((2 * H, H), F32)
    for k in (3, 7, 11, 15):
        p_out[k, 16:32, :] = jnp.zeros((16, H), BF16)

    pl.semaphore_wait(barrier, len(peers))
    halo_copies = [
        remote(
            nodes_ref.at[pl.ds(0, border), :],
            halo_ref.at[7 - k],
            near_sem.at[0, k],
            near_sem.at[1, 7 - k],
            peer,
        )
        for k, peer in enumerate(near)
    ]
    for copy in halo_copies:
        copy.start()

    def column(ref, c, size):
        rows = size // 128
        return jnp.concatenate(
            [
                jnp.broadcast_to(ref[pl.ds(c * rows + k, 1), :], (128, 128)).T.astype(jnp.int16)
                for k in range(rows)
            ],
            axis=0,
        )

    def hot_rows(col, first, n):
        size = col.shape[0]
        lane = lax.broadcasted_iota(jnp.int32, (size, 128), 1).astype(jnp.int16)
        one, zero = jnp.ones((size, 128), BF16), jnp.zeros((size, 128), BF16)
        return [
            jnp.where(col == lane + jnp.int16(first + k * 128), one, zero)
            for k in range(n // 128)
        ]

    def hot_cols(ref, c, size, n):
        rows = size // 128
        down = lax.broadcasted_iota(jnp.int32, (n, 128), 0).astype(jnp.int16)
        one, zero = jnp.ones((n, 128), BF16), jnp.zeros((n, 128), BF16)
        return jnp.concatenate(
            [
                jnp.where(
                    jnp.broadcast_to(ref[pl.ds(c * rows + k, 1), :], (n, 128)).astype(jnp.int16)
                    == down,
                    one,
                    zero,
                )
                for k in range(rows)
            ],
            axis=1,
        )

    loads[3].wait()
    loads[5].wait()

    def local_part(c, carry):
        at = pl.ds(pl.multiple_of(c * WIDE, WIDE), WIDE)
        col = column(sidx_ref, c, WIDE)
        hot_s = hot_rows(col, 0, n_p)
        hot_h = hot_rows(col, n_p, n_h)
        hot_r = hot_rows(column(recv_ref, c, WIDE), 0, n_p)
        hot_ref[at, :] = jnp.concatenate(hot_h + hot_r, axis=1)
        z1_ref[at, :] = dot(
            jnp.concatenate(hot_s + hot_r + [edges_ref[at, :]], axis=1), table_ref[0:n_l, :]
        )
        return carry

    lax.fori_loop(0, n_e // WIDE, local_part, 0)

    for copy in halo_copies:
        copy.wait()
    halo = halo_ref[...].reshape(n_h, H)
    table_ref[n_l:, :] = dot(halo, w_ei_ref[0:H, :]).astype(BF16)
    loads[6].wait()
    count = count_ref[0]

    def forward(c, carry):
        at = pl.ds(pl.multiple_of(c * CHUNK, CHUNK), CHUNK)
        z1 = z1_ref[at, :] + dot(hot_ref[at, 0:n_h], table_ref[n_l:, :])
        a1, sp = silu_parts(z1)
        a1 = a1.astype(BF16)
        a1_ref[at, :] = a1
        sp_ref[at, :] = sp
        centre = dot(jnp.concatenate([a1, a1], axis=1), weo_ref[...])
        r2 = lax.rsqrt(mean_row(centre * centre) + EPS)
        where = c * CHUNK + lax.broadcasted_iota(jnp.int32, (CHUNK, 1), 0)
        r2 = jnp.where(where < count, r2, 0.0)
        n2 = centre * r2
        n2_ref[at, :] = n2
        r2_ref[at, :] = jnp.broadcast_to(r2, (CHUNK, 128))
        new_edges_ref[at, :] = (edges_ref[at, :].astype(F32) + n2).astype(BF16)
        agg_ref[...] += dot(hot_cols(recv_ref, c, CHUNK, n_p), n2.astype(BF16))
        return carry

    lax.fori_loop(0, n_e // CHUNK, forward, 0)

    stores = [pltpu.make_async_copy(new_edges_ref, new_edges_hbm, store_sem.at[0])]
    stores[0].start()
    for k in (7, 8, 9):
        loads[k].wait()
    joined = jnp.concatenate([nodes, agg_ref[...].astype(BF16)], axis=1)
    a3, sp3 = silu_parts(dot(joined, w_ni_ref[...]))
    a3 = a3.astype(BF16)
    z4 = dot(a3, w_no_ref[...])
    centre = z4 - mean_row(z4)
    r4 = lax.rsqrt(mean_row(centre * centre) + EPS)
    n4 = centre * r4
    new_nodes_ref[...] = (nodes.astype(F32) + n4).astype(BF16)
    ncot = ncot_ref[...].astype(F32)
    dz4 = (r4 * (ncot - mean_row(ncot) - n4 * mean_row(ncot * n4))).astype(BF16)
    dz3 = (dot_nt(dz4, w_no_ref[...]) * sp3).astype(BF16)
    d_joined = dot_nt(dz3, w_ni_ref[...])
    dagg_ref[...] = d_joined[:, H:].astype(BF16)
    node_grad_ref[...] = ncot + d_joined[:, :H]
    part_ref[4 * H : 6 * H, :] = dot_tn(joined, dz3)
    part_ref[6 * H : 7 * H, :] = dot_tn(a3, dz4)
    stores.append(pltpu.make_async_copy(new_nodes_ref, new_nodes_hbm, store_sem.at[1]))
    stores[1].start()
    loads[10].wait()

    def backward(c, carry):
        at = pl.ds(pl.multiple_of(c * CHUNK, CHUNK), CHUNK)
        n2 = n2_ref[at, :]
        g = cot_ref[at, :].astype(F32) + dot(hot_ref[at, n_h:], dagg_ref[...])
        dz2 = (r2_ref[at, :] * (g - mean_row(g) - n2 * mean_row(g * n2))).astype(BF16)
        dz1 = (dot_nt(dz2, w_eo_ref[...]) * sp_ref[at, :]).astype(BF16)
        part_ref[2 * H : 3 * H, :] += dot_tn(edges_ref[at, :], dz1)
        part_ref[3 * H : 4 * H, :] += dot_tn(a1_ref[at, :], dz2)
        hot = jnp.concatenate(
            [hot_cols(sidx_ref, c, CHUNK, n_p + n_h), hot_cols(recv_ref, c, CHUNK, n_p)], axis=0
        )
        gsum_ref[...] += dot(hot, dz1)
        return carry

    lax.fori_loop(0, n_e // CHUNK, backward, 0)

    g_s = gsum_ref[0:n_p, :].astype(BF16)
    g_h = gsum_ref[n_p : n_p + n_h, :].astype(BF16)
    g_r = gsum_ref[n_p + n_h :, :].astype(BF16)
    w_s, w_r = w_ei_ref[0:H, :], w_ei_ref[H : 2 * H, :]
    part_ref[0:H, :] = dot_tn(nodes, g_s) + dot_tn(halo, g_h)
    part_ref[H : 2 * H, :] = dot_tn(nodes, g_r)

    half = c_out.shape[0]
    part = half // 4

    def chip_rows(dx, base):
        return pl.ds(pl.multiple_of(base * half + lax.rem(my_x + dx, 4) * part, 16), part)

    core = {}
    for k, dx in enumerate(SHIFTS):
        rows = chip_rows(dx, 0)
        c_out[rows, :] = part_ref[chip_rows(dx, 1 - my_c), :].astype(BF16)
        core[dx] = remote(
            c_out.at[rows, :], c_land.at[rows, :], send_sem.at[54 + k], recv_sem.at[54 + k], mate
        )
        core[dx].start()
    owed_ref[...] = dot_nt(g_h, w_s).astype(BF16).reshape(8, border, H)
    returned = [
        remote(owed_ref.at[k], back_ref.at[7 - k], near_sem.at[2, k], near_sem.at[3, 7 - k], peer)
        for k, peer in enumerate(near)
    ]
    node_grad_ref[...] += dot_nt(g_s, w_s) + dot_nt(g_r, w_r)
    def share(src, dst, base, row):
        copies = [
            remote(src(d), dst(d), send_sem.at[base + d], recv_sem.at[base + d], peer)
            for d, peer in enumerate(row, 1)
        ]
        for copy in copies:
            copy.start()
        return copies

    my_p = my_x * 4 + my_y
    copies = {}
    for dx in SHIFTS:
        core[dx].wait()
        total = part_ref[chip_rows(dx, my_c), :] + c_land[chip_rows(dx, 0), :].astype(F32)
        for k, (low, size) in enumerate(PIECES[0:4]):
            p_out[lax.rem(my_x + dx, 4) * 4 + k, 0:size, :] = total[low : low + size, :].astype(BF16)
        for d in range(max(dx * 4, 1), dx * 4 + 4):
            copies[d] = remote(
                p_out.at[plane[d - 1][0] * 4 + plane[d - 1][1]],
                p_land.at[d - 1],
                send_sem.at[d],
                recv_sem.at[d],
                plane_row[d - 1],
            )
            copies[d].start()
    for copy in returned:
        copy.start()
    acc = p_out[my_p].astype(F32)
    for d in FROM_NEAR:
        copies[d].wait()
        acc = acc + p_land[d - 1].astype(F32)

    z_out[...] = acc.astype(BF16)
    copies = share(lambda d: z_out, lambda d: z_land.at[my_z], 15, row_z)
    z_land[my_z] = z_out[...]

    for copy in returned:
        copy.wait()
    back = back_ref[0].astype(F32)
    for k in range(1, 8):
        back = back + back_ref[k].astype(F32)
    node_grad_ref[0:border, :] += back
    stores.append(pltpu.make_async_copy(node_grad_ref, node_grad_hbm, store_sem.at[2]))
    stores[2].start()

    for copy in copies:
        copy.wait()
    acc = z_land[0].astype(F32)
    for k in range(1, 8):
        acc = acc + z_land[k].astype(F32)

    def pass_on(k, p):
        piece = all_ref.at[my_c, p]
        copy = remote(piece, piece, send_sem.at[38 + k], recv_sem.at[38 + k], mate)
        copy.start()
        return copy

    all_ref[my_c, my_p] = acc.astype(BF16)
    copies = share(
        lambda d: all_ref.at[my_c, my_p], lambda d: all_ref.at[my_c, my_p], 22, plane_row
    )
    passed = [pass_on(0, my_p)]
    for d in FROM_NEAR:
        copies[d - 1].wait()
        passed.append(pass_on(d, origin[d - 1][0] * 4 + origin[d - 1][1]))
    for copy in passed:
        copy.wait()
    stores.append(pltpu.make_async_copy(all_ref, total_hbm, store_sem.at[3]))
    stores[3].start()
    for store in stores:
        store.wait()


def vmem():
    return pl.BlockSpec(memory_space=pltpu.VMEM)


def hbm():
    return pl.BlockSpec(memory_space=pltpu.HBM)


def anywhere():
    return pl.BlockSpec(memory_space=pl.ANY)


def step_call(sizes, args):
    n_p, n_e = args[0].shape[0], args[1].shape[0]
    border = n_p // 8
    n_h = 8 * border
    half = 7 * H // 2
    dma = pltpu.SemaphoreType.DMA
    return pl.pallas_call(
        functools.partial(step_kernel, sizes),
        out_shape=(
            jax.ShapeDtypeStruct((n_p, H), BF16),
            jax.ShapeDtypeStruct((n_e, H), BF16),
            jax.ShapeDtypeStruct((n_p, H), F32),
            jax.ShapeDtypeStruct((2, 16, 32, H), BF16),
        ),
        in_specs=[hbm()] * 11,
        out_specs=[hbm()] * 4,
        scratch_shapes=[
            pltpu.SMEM(a.shape, a.dtype) if a.shape == (1,) else pltpu.VMEM(a.shape, a.dtype)
            for a in args
        ]
        + [
            dma((11,)),
            pltpu.VMEM((n_p, H), BF16),
            pltpu.VMEM((n_e, H), BF16),
            pltpu.VMEM((n_p, H), F32),
            dma((4,)),
            pltpu.VMEM((8, border, H), BF16),
            pltpu.VMEM((8, border, H), BF16),
            pltpu.VMEM((8, border, H), BF16),
            dma((4, 8)),
            pltpu.VMEM((2 * n_p + H + n_h, H), BF16),
            pltpu.VMEM((n_e // 128, 128), jnp.int32),
            pltpu.VMEM((2 * H, H), BF16),
            pltpu.VMEM((n_e, n_h + n_p), BF16),
            pltpu.VMEM((n_e, H), F32),
            pltpu.VMEM((n_e, H), BF16),
            pltpu.VMEM((n_e, H), F32),
            pltpu.VMEM((n_e, H), F32),
            pltpu.VMEM((n_e, H), F32),
            pltpu.VMEM((n_p, H), F32),
            pltpu.VMEM((n_p, H), BF16),
            pltpu.VMEM((2 * n_p + n_h, H), F32),
            pltpu.VMEM((7 * H, H), F32),
            pltpu.VMEM((half, H), BF16),
            pltpu.VMEM((half, H), BF16),
            pltpu.VMEM((16, 32, H), BF16),
            pltpu.VMEM((15, 32, H), BF16),
            pltpu.VMEM((32, H), BF16),
            pltpu.VMEM((8, 32, H), BF16),
            pltpu.VMEM((2, 16, 32, H), BF16),
            dma((58,)),
            dma((58,)),
        ],
        compiler_params=pltpu.CompilerParams(
            collective_id=0, has_side_effects=True, vmem_limit_bytes=62_000_000
        ),
    )(*args)


def finish_kernel(
    factor,
    nn_ref,
    ne_ref,
    ng_ref,
    total_ref,
    nn_out,
    ne_out,
    ng_out,
    ei_out,
    eo_out,
    ni_out,
    no_out,
    nn_buf,
    ne_buf,
    ng_buf,
    total_buf,
    grad_buf,
    in_sem,
    out_sem,
):
    quarter = ne_buf.shape[0] // 4
    parts = [pl.ds(k * quarter, quarter) for k in range(4)]
    brought = [pltpu.make_async_copy(total_ref, total_buf, in_sem.at[0])]
    for k, part in enumerate(parts):
        brought.append(
            pltpu.make_async_copy(ne_ref.at[part, :], ne_buf.at[part, :], in_sem.at[1 + k])
        )
    brought.append(pltpu.make_async_copy(ng_ref, ng_buf, in_sem.at[5]))
    brought.append(pltpu.make_async_copy(nn_ref, nn_buf, in_sem.at[6]))
    for copy in brought:
        copy.start()
    taken = []

    def take(src, dst):
        taken.append(pltpu.make_async_copy(src, dst, out_sem.at[len(taken)]))
        taken[-1].start()

    brought[0].wait()
    half = grad_buf.shape[0] // 2
    for c in range(2):
        for k, (low, size) in enumerate(PIECES):
            rows = pl.ds(c * half + low, size)
            grad_buf[rows, :] = total_buf[c, k, 0:size, :].astype(F32) * factor
    first = 0
    for out in (ei_out, eo_out, ni_out, no_out):
        take(grad_buf.at[pl.ds(first, out.shape[0]), :], out)
        first += out.shape[0]
    for k, part in enumerate(parts):
        brought[1 + k].wait()
        take(ne_buf.at[part, :], ne_out.at[part, :])
    brought[5].wait()
    take(ng_buf, ng_out)
    brought[6].wait()
    take(nn_buf, nn_out)
    for copy in taken:
        copy.wait()


def finish_call(factor, new_nodes, new_edges, node_grad, total):
    shapes = [
        (new_nodes.shape, BF16),
        (new_edges.shape, BF16),
        (node_grad.shape, F32),
        ((3 * H, H), F32),
        ((H, H), F32),
        ((2 * H, H), F32),
        ((H, H), F32),
    ]
    return pl.pallas_call(
        functools.partial(finish_kernel, factor),
        out_shape=tuple(jax.ShapeDtypeStruct(s, t) for s, t in shapes),
        in_specs=[hbm()] * 4,
        out_specs=[hbm()] * 7,
        scratch_shapes=[
            pltpu.VMEM(new_nodes.shape, BF16),
            pltpu.VMEM(new_edges.shape, BF16),
            pltpu.VMEM(node_grad.shape, F32),
            pltpu.VMEM(total.shape, BF16),
            pltpu.VMEM((7 * H, H), F32),
            pltpu.SemaphoreType.DMA((7,)),
            pltpu.SemaphoreType.DMA((10,)),
        ],
        compiler_params=pltpu.CompilerParams(vmem_limit_bytes=62_000_000),
    )(new_nodes, new_edges, node_grad, total)


def shards(
    node_latents,
    edge_latents,
    senders,
    receivers,
    edge_count,
    w_edge_in,
    w_edge_out,
    w_node_in,
    w_node_out,
    node_cotangent,
    edge_cotangent,
):
    count_e = edge_latents.shape[0]
    sizes = (lax.axis_size("strip"), lax.axis_size("sub"))
    factor = 1.0 / math.sqrt(count_e * sizes[0] * sizes[1])
    return finish_call(
        factor,
        *step_call(
            sizes,
            (
                node_latents,
                edge_latents,
                senders.reshape(count_e // 128, 128),
                receivers.reshape(count_e // 128, 128),
                edge_count,
                w_edge_in,
                w_edge_out,
                w_node_in,
                w_node_out,
                node_cotangent,
                edge_cotangent,
            ),
        )
    )


def solution(mesh):
    placed = (
        P(("strip", "sub"), None),
        P(("strip", "sub"), None),
        P(("strip", "sub")),
        P(("strip", "sub")),
        P(("strip", "sub")),
        P(),
        P(),
        P(),
        P(),
        P(("strip", "sub"), None),
        P(("strip", "sub"), None),
    )
    return jax.shard_map(
        shards,
        mesh=mesh,
        in_specs=placed,
        out_specs=(
            P(("strip", "sub"), None),
            P(("strip", "sub"), None),
            P(("strip", "sub"), None),
            P(),
            P(),
            P(),
            P(),
        ),
        check_vma=False,
    )
```
